256 devices in a mesh: wave: 32 (over z, x_lo, core), depth: 8 (over x_hi, y).
Axes of the slice: x: 4 (x_hi: 2, x_lo: 2; x = x_hi * 2 + x_lo), y: 4, z: 8, core: 2. Of those that a mesh axis runs over, the one named last changes fastest.
Arguments:
- slip_field: bfloat16 [16, 2, 1024, 1024], P('depth', None, 'wave'), may hold values from -6 to 6
- slip_mask: int32 [16, 32, 32], P('depth', 'wave'), may hold values 0 or 1
- slice_layer: int32 [64], replicated, may hold values from 0 to 15, as said below
- layer_material: int32 [16], replicated, may hold values from 0 to 7
- materials: float32 [3, 8], replicated, may hold values from 0.3 to 1
Outputs:
- coulomb_change: float32 [8, 1024, 1024], P('depth', 'wave')
The draws below stay inside these ranges and needn't reach their ends.
Inputs may be any that keep to these rules, and one draw needn't show every extreme that they name: `slice_layer`: never falls along the column; 0 at the first slice and 15 at the last.
All inputs are finite; a program needn't handle non-finite values. No bound on the sum of `slip_mask` on one device may be relied on, other than what follows from the above.
Results may differ from the reference program's by a relative error of at most 0.0015.
Values may be sent and summed in bfloat16 or wider, within the bound.
A program may use at most 64 MiB of HBM per device.

```python
import math
import jax
import jax.numpy as jnp
from jax import lax

GRID = 1024
NZ = 64
S = 16
R = 8
NL = 16
NM = 8
TILE = 32


def draw_slice_layer(key, part):
    coins = jax.random.randint(jax.random.fold_in(key, 7), (NZ,), 0, 3)
    places = jnp.arange(NZ, dtype=jnp.int32)
    rises = jnp.where((coins == 0) & (places > 0), 1, 0).astype(jnp.int32)
    layers = jnp.minimum(jnp.cumsum(rises), NL - 1)
    return jnp.where(places == NZ - 1, NL - 1, layers).astype(jnp.int32)


def touch_ends(values, stream_key, low, high):
    shape = values.shape
    place = [jax.random.randint(jax.random.fold_in(stream_key, axis), (), 0, shape[axis]) for axis in range(len(shape))]
    values = values.at[tuple(place)].set(low)
    longest = shape.index(max(shape))
    place[longest] = (place[longest] + 1) % shape[longest]
    return values.at[tuple(place)].set(high)


def block_scale(own_key, dims, pieces, least, high):
    def one(axis_at, shards_of):
        heights = jax.random.uniform(jax.random.fold_in(jax.random.fold_in(own_key, 6), axis_at), (shards_of,), jnp.float32, least / len(pieces), high / len(pieces))
        return jnp.repeat(jnp.exp(heights), dims[axis_at] // shards_of).reshape((-1,) + (1,) * (len(dims) - axis_at - 1))

    loudness = one(*pieces[0])
    for cut in pieces[1:]:
        loudness = loudness * one(*cut)
    return loudness


def bell_draw(own_key, shape, scale, reach, pieces=(), kind=jnp.bfloat16):
    loudness = block_scale(own_key, shape, pieces, -0.22, 0.18) if pieces else 1.0
    array = jax.random.normal(own_key, shape, jnp.float32) * scale * loudness
    return jnp.minimum(jnp.maximum(array, -reach), reach).astype(kind)


def setup_inputs(seed: int = 0) -> dict:
    splits = jax.random.split(jax.random.key(seed), 6)
    slip_field = bell_draw(splits[0], (S, 2, GRID, GRID), 1.0, 6.0, ((0, 8), (2, 32)))
    slip_mask = touch_ends((jax.random.randint(splits[1], (S, GRID // TILE, GRID // TILE), 0, 3) < 2).astype(jnp.int32), jax.random.fold_in(splits[1], 1), 0, 1)
    slice_layer = draw_slice_layer(jax.random.fold_in(splits[5], 71), 0)
    layer_material = touch_ends(jax.random.randint(splits[3], (NL,), 0, NM), jax.random.fold_in(splits[3], 1), 0, NM - 1).astype(jnp.int32)
    materials = jnp.clip(jax.random.uniform(splits[4], (3, NM), jnp.float32, 0.3, 1.0), 0.3, 1.0)
    return {"slip_field": slip_field, "slip_mask": slip_mask, "slice_layer": slice_layer, "layer_material": layer_material, "materials": materials}


slice_thick = 0.1

def signed_index(length):
    ladder = jnp.arange(length, dtype=jnp.int32)
    return ((ladder + length // 2) % length - length // 2).astype(jnp.float32)

def reference(slip_field, slip_mask, slice_layer, layer_material, materials):
    layer_kinds = layer_material[slice_layer]
    properties = materials[:, layer_kinds]
    thickness = slice_thick * properties[0]
    center = jnp.cumsum(thickness) - 0.5 * thickness
    source_at = jnp.arange(S, dtype=jnp.int32) * (NZ // S) + NZ // (4 * S)
    receiver_at = jnp.arange(R, dtype=jnp.int32) * (NZ // R) + NZ // (2 * R) - 1
    source_depth = center[source_at]
    receiver_depth = center[receiver_at]
    rigidity = properties[1][receiver_at]
    friction = properties[2][receiver_at]
    tile_size = GRID // slip_mask.shape[1]
    cells_mask = jnp.repeat(jnp.repeat(slip_mask, tile_size, axis=1), tile_size, axis=2).astype(jnp.float32)

    def forward(source_index):
        source_cells = slip_field[source_index].astype(jnp.float32) * cells_mask[source_index][None]
        spectrum = jnp.fft.fft2(source_cells, norm='ortho')
        return (jnp.real(spectrum).astype(jnp.bfloat16), jnp.imag(spectrum).astype(jnp.bfloat16))
    spec_real, spec_imag = lax.map(forward, jnp.arange(S, dtype=jnp.int32))
    x_wave = signed_index(GRID)[:, None]
    y_wave = signed_index(GRID)[None, :]
    magnitude = jnp.sqrt(x_wave * x_wave + y_wave * y_wave)
    bounded = jnp.maximum(magnitude, 1.0)
    wave_num = 2.0 * math.pi / GRID * magnitude
    along_x = x_wave / bounded
    along_y = y_wave / bounded

    def receiver(receiver_index):
        depth_here = receiver_depth[receiver_index]

        def add_source(running, source_index):
            acc_real, acc_imag = running
            first_real = spec_real[source_index, 0].astype(jnp.float32)
            second_real = spec_real[source_index, 1].astype(jnp.float32)
            first_imag = spec_imag[source_index, 0].astype(jnp.float32)
            second_imag = spec_imag[source_index, 1].astype(jnp.float32)
            near_gap = jnp.abs(depth_here - source_depth[source_index])
            far_sum = depth_here + source_depth[source_index]
            direct = jnp.exp(-wave_num * near_gap)
            mirror = jnp.exp(-wave_num * far_sum)
            summed = direct + mirror
            slope_term = wave_num * (near_gap * direct - far_sum * mirror)
            strike = summed - along_x * along_x * slope_term
            cross_term = -along_x * along_y * slope_term
            dipping = summed - along_y * along_y * slope_term
            normal_part = summed - slope_term
            add_real = jnp.stack([strike * first_real + cross_term * second_real, cross_term * first_real + dipping * second_real, -normal_part * (along_x * first_imag + along_y * second_imag)])
            add_imag = jnp.stack([strike * first_imag + cross_term * second_imag, cross_term * first_imag + dipping * second_imag, normal_part * (along_x * first_real + along_y * second_real)])
            return ((acc_real + add_real, acc_imag + add_imag), None)
        empty_sum = jnp.zeros((3, GRID, GRID), jnp.float32)
        totals = lax.scan(add_source, (empty_sum, empty_sum), jnp.arange(S, dtype=jnp.int32))[0]
        weights = jnp.stack([rigidity[receiver_index], rigidity[receiver_index], rigidity[receiver_index] * friction[receiver_index]])
        scaled = lax.complex(totals[0] * weights[:, None, None], totals[1] * weights[:, None, None])
        stress = jnp.real(jnp.fft.ifft2(scaled, norm='ortho'))
        return jnp.sqrt(stress[0] * stress[0] + stress[1] * stress[1] + 1.0) + stress[2]
    return lax.map(receiver, jnp.arange(R, dtype=jnp.int32))
```

```python
import functools
import math

import jax
import jax.numpy as jnp
import ml_dtypes
import numpy as np
from jax import lax
from jax.experimental import pallas as pl
from jax.experimental.pallas import tpu as pltpu
from jax.sharding import PartitionSpec as P

GRID = 1024
HALF = 512
QUARTER = 256
S = 16
R = 8
NZ = 64
DEVICES = 256
BF16 = jnp.bfloat16
F32 = jnp.float32
VMEM = pltpu.VMEM
SMEM = pltpu.SMEM


def split_table(table):
    high = table.astype(ml_dtypes.bfloat16)
    low = (table - high.astype(np.float64)).astype(ml_dtypes.bfloat16)
    return np.stack([high, low])


def tables():
    j = np.arange(QUARTER, dtype=np.int64)[:, None]
    cell = np.arange(HALF, dtype=np.int64)[None, :]
    rows = []
    for parity in range(2):
        angle = 2.0 * np.pi * (((2 * j + parity) * cell) % GRID) / GRID
        real, imag = np.cos(angle), -np.sin(angle)
        if parity == 0:
            imag[0] = 1.0 - 2.0 * (cell[0] % 2)
        rows += [real, imag]
    real_dft = np.concatenate(rows) / 32.0
    k = np.arange(QUARTER, dtype=np.int64)
    angle = 2.0 * np.pi * ((k[:, None] * k[None, :]) % QUARTER) / QUARTER
    cosine, sine = np.cos(angle) / 32.0, np.sin(angle) / 32.0
    complex_dft = np.block([[cosine, -sine], [sine, cosine]])
    turn = 2.0 * np.pi * np.arange(4)[:, None] * k[None, :] / GRID
    twiddle = np.concatenate([np.cos(turn), -np.sin(turn)]).astype(np.float32)
    return split_table(real_dft), split_table(complex_dft), twiddle


def halves(value):
    high = value.astype(BF16)
    return high, (value - high.astype(F32)).astype(BF16)


def dot(left, right, transposed=False):
    dims = (((1,), (1 if transposed else 0,)), ((), ()))
    return lax.dot_general(left, right, dims, preferred_element_type=F32)


def forward_rows(mask_ref, slip_ref, table_ref, out_ref):
    tile = lax.broadcasted_iota(jnp.int32, (32, GRID), 0)
    cell = lax.broadcasted_iota(jnp.int32, (32, GRID), 1)
    spread = (cell // 32 == tile).astype(BF16)
    mask = dot(mask_ref[...].astype(F32).astype(BF16), spread)
    slip = slip_ref[...].astype(F32)
    rows = slip.shape[0] // 2
    cells = jnp.concatenate([slip[:rows] * mask[0:1], slip[rows:] * mask[1:2]], axis=0)
    near, far = cells[:, :HALF], cells[:, HALF:]
    for parity, combined in enumerate((near + far, near - far)):
        high, low = halves(combined)
        part = slice(parity * HALF, (parity + 1) * HALF)
        result = (
            dot(table_ref[0, part], high, True)
            + dot(table_ref[0, part], low, True)
            + dot(table_ref[1, part], high, True)
        )
        for imag in range(2):
            out_ref[pl.ds(2 * parity + imag, QUARTER, stride=4), :] = result[
                imag * QUARTER : (imag + 1) * QUARTER
            ]


def swap_groups(items):
    lane = lax.broadcasted_iota(jnp.int32, items[0].shape, 1)
    for width in (2, 1):
        size = 32 * width
        upper = (lane // size) % 2 == 1
        out = list(items)
        for a in range(4):
            if a & width:
                continue
            b = a | width
            first, second = items[a], items[b]
            out[a] = jnp.where(upper, pltpu.roll(second, size, 1), first)
            out[b] = jnp.where(upper, second, pltpu.roll(first, 128 - size, 1))
        items = out
    return items


def radix_four(items):
    (r0, i0), (r1, i1), (r2, i2), (r3, i3) = items
    ar, ai, br, bi = r0 + r2, i0 + i2, r0 - r2, i0 - i2
    cr, ci, dr, di = r1 + r3, i1 + i3, r1 - r3, i1 - i3
    return [
        (ar + cr, ai + ci),
        (br + di, bi - dr),
        (ar - cr, ai - ci),
        (br - di, bi + dr),
    ]


def times(item, cosine, sine):
    real, imag = item
    return real * cosine - imag * sine, real * sine + imag * cosine


def depths(slice_ref, layer_ref, material_ref):
    center, rigidity, friction = [], [], []
    top = None
    for place in range(NZ):
        kind = layer_ref[slice_ref[place]]
        thickness = jnp.float32(0.1) * material_ref[kind]
        top = thickness if top is None else top + thickness
        center.append(top - 0.5 * thickness)
        if place % 8 == 3:
            rigidity.append(material_ref[8 + kind])
            friction.append(material_ref[16 + kind])
    source = [center[4 * s + 1] for s in range(S)]
    receiver = [center[8 * r + 3] for r in range(R)]
    return source, receiver, rigidity, friction


def geometry(first_row, rows, half, ky):
    k0 = lax.broadcasted_iota(jnp.int32, (rows, 128), 0) % 4
    k1 = lax.broadcasted_iota(jnp.int32, (rows, 128), 1) + 128 * half
    kx = 4 * k1 + k0
    signed = jnp.where(kx >= HALF, kx - GRID, kx)
    x_wave, y_wave = signed.astype(F32), ky.astype(F32)
    magnitude = jnp.sqrt(x_wave * x_wave + y_wave * y_wave)
    bounded = jnp.maximum(magnitude, 1.0)
    along_x, along_y = x_wave / bounded, y_wave / bounded
    x_edge, y_edge = signed == -HALF, ky == -HALF
    cross = jnp.where(x_edge != y_edge, 0.0, along_x * along_y)
    odd_x = jnp.where(x_edge, 0.0, along_x)
    odd_y = jnp.where(y_edge, 0.0, along_y)
    wave = 2.0 * math.pi / GRID * magnitude
    return wave, along_x * along_x, cross, along_y * along_y, odd_x, odd_y


def middle(
    position,
    slice_ref,
    layer_ref,
    material_ref,
    table_ref,
    twiddle_ref,
    got_ref,
    out_ref,
    left_ref,
    spec_ref,
    edge_ref,
    suffix_ref,
    trac_ref,
):
    j = position()
    first = j == 0
    source, receiver, rigidity, friction = depths(slice_ref, layer_ref, material_ref)
    keep_imag = jnp.where(first, 0.0, 1.0).astype(F32)
    only_first = 1.0 - keep_imag
    cosines = [twiddle_ref[a : a + 1, :] for a in range(4)]
    sines = [twiddle_ref[4 + a : 5 + a, :] for a in range(4)]

    loaded = [got_ref[pl.ds(c, DEVICES, stride=4), :] for c in range(4)]
    blocks = [[[None] * 8 for _ in range(4)] for _ in range(4)]
    for c in range(4):
        for outer in range(8):
            group = swap_groups([loaded[c][(4 * outer + inner) * 8 : (4 * outer + inner) * 8 + 8] for inner in range(4)])
            for g in range(4):
                blocks[c][g][outer] = group[g]
    for g in range(4):
        whole = [
            [jnp.concatenate([blocks[c][g][2 * x0], blocks[c][g][2 * x0 + 1]], axis=1) for x0 in range(4)]
            for c in range(4)
        ]
        kinds = [
            [(whole[0][x0], whole[1][x0] * keep_imag) for x0 in range(4)],
            [(whole[2][x0], whole[3][x0]) for x0 in range(4)],
            [(whole[1][x0], jnp.zeros_like(whole[1][x0])) for x0 in range(4)],
        ]
        for p in range(3):
            mixed = radix_four(kinds[p])
            for k0 in range(4):
                real, imag = times(mixed[k0], cosines[k0], sines[k0])
                if p < 2:
                    place = pl.ds(64 * g + 4 * p + k0, 8, stride=8)
                else:
                    place = pl.ds(256 + 32 * g + k0, 8, stride=4)
                for t in range(2):
                    left_ref.at[t][place, :] = real[:, 128 * t : 128 * t + 128]
                    left_ref.at[2 + t][place, :] = imag[:, 128 * t : 128 * t + 128]
    high, low = halves(jnp.concatenate([left_ref[t] for t in range(4)], axis=1))
    spectra = dot(high, table_ref[0]) + dot(low, table_ref[0]) + dot(high, table_ref[1])
    spec_ref[...] = spectra.astype(BF16).astype(F32)

    def unit(rows, base, step, half, ky, row_weight, write):
        wave, uu, uv, vv, odd_x, odd_y = geometry(0, rows, half, ky)

        def fields(s):
            picked = []
            for q in range(2):
                row = base + (2 * (s % 2) + q) * 8 * step + (s // 2) * step
                for imag in range(2):
                    start = 256 * imag + 128 * half
                    picked.append(spec_ref[row : row + rows, start : start + 128])
            return picked

        zero = jnp.zeros((rows, 128), F32)
        suffix, moment = [zero] * 4, [zero] * 4
        for s in reversed(range(S)):
            decay = jnp.exp(-wave * source[s])
            values = fields(s)
            scaled = [decay * value for value in values]
            suffix = [a + b for a, b in zip(suffix, scaled)]
            moment = [a + source[s] * b for a, b in zip(moment, scaled)]
            if s % 2 == 1:
                for n in range(4):
                    suffix_ref[s // 2, n, 0:rows, :] = suffix[n]
                    suffix_ref[s // 2, 4 + n, 0:rows, :] = moment[n]
        total, total_moment = suffix, moment
        prefix, moment = [zero] * 4, [zero] * 4
        for s in range(S - 1):
            growth = jnp.exp(wave * source[s])
            values = fields(s)
            scaled = [growth * value for value in values]
            prefix = [a + b for a, b in zip(prefix, scaled)]
            moment = [a + source[s] * b for a, b in zip(moment, scaled)]
            if s % 2 == 0:
                r = s // 2
                z = receiver[r]
                fall, rise = jnp.exp(-wave * z), jnp.exp(wave * z)
                summed, slope = [], []
                for n in range(4):
                    after, after_moment = suffix_ref[r, n, 0:rows, :], suffix_ref[r, 4 + n, 0:rows, :]
                    summed.append(fall * (prefix[n] + total[n]) + rise * after)
                    slope.append(
                        wave
                        * (
                            fall * (z * (prefix[n] - total[n]) - (moment[n] + total_moment[n]))
                            + rise * (after_moment - z * after)
                        )
                    )
                weight = row_weight * rigidity[r]
                along = [a - b for a, b in zip(summed, slope)]
                write(
                    r,
                    [
                        weight * (summed[0] - uu * slope[0] - uv * slope[2]),
                        weight * (summed[1] - uu * slope[1] - uv * slope[3]),
                        weight * (summed[2] - uv * slope[0] - vv * slope[2]),
                        weight * (summed[3] - uv * slope[1] - vv * slope[3]),
                        -weight * friction[r] * (odd_x * along[1] + odd_y * along[3]),
                        weight * friction[r] * (odd_x * along[0] + odd_y * along[2]),
                    ],
                )

    for half in range(2):

        def write_edge(r, values):
            for n in range(6):
                edge_ref[r, n] = values[n] * only_first

        unit(4, 256, 4, half, jnp.full((4, 128), -HALF, jnp.int32), jnp.ones((4, 128), F32), write_edge)

        def write_main(r, values):
            for c in range(3):
                real, imag = values[2 * c], values[2 * c + 1]
                pad = jnp.zeros((4, 128), F32)
                real = real - jnp.concatenate([edge_ref[r, 2 * c + 1], pad], axis=0)
                imag = imag + jnp.concatenate([edge_ref[r, 2 * c], pad], axis=0)
                place = pl.ds(64 * c + r, 8, stride=8)
                trac_ref.at[half][place, :] = real
                trac_ref.at[2 + half][place, :] = -imag

        kind = lax.broadcasted_iota(jnp.int32, (8, 128), 0) // 4
        weight = jnp.where(kind == 0, 1.0 + keep_imag, 2.0).astype(F32)
        unit(8, 0, 8, half, 2 * j + kind, weight, write_main)

    high, low = halves(jnp.concatenate([trac_ref[t] for t in range(4)], axis=1))
    turned = dot(high, table_ref[0]) + dot(low, table_ref[0]) + dot(high, table_ref[1])
    for c in range(3):
        fields = []
        for p in range(2):
            items = []
            for k0 in range(4):
                row = 64 * c + 32 * p + 8 * k0
                items.append(times((turned[row : row + 8, :256], turned[row : row + 8, 256:]), cosines[k0], sines[k0]))
            mixed = radix_four(items)
            fields.append([item[0] for item in mixed])
            fields.append([-item[1] for item in mixed])
        for outer in range(8):
            cut = slice(128 * (outer % 2), 128 * (outer % 2) + 128)
            group = swap_groups([fields[n][outer // 2][:, cut] for n in range(4)])
            for inner in range(4):
                w = 4 * outer + inner
                out_ref[pl.ds(24 * w + c, 8, stride=3), :] = group[inner]


def inverse_rows(table_ref, got_ref, out_ref):
    flipped = [got_ref[pl.ds(c, DEVICES, stride=3), :].T for c in range(3)]
    parts = []
    for parity in range(2):
        rows = []
        for c in range(3):
            real = flipped[c][64 * parity : 64 * parity + 32]
            imag = flipped[c][64 * parity + 32 : 64 * parity + 64]
            rows.append(jnp.concatenate([real, imag], axis=1))
        high, low = halves(jnp.concatenate(rows, axis=0))
        part = slice(parity * HALF, (parity + 1) * HALF)
        parts.append(
            dot(high, table_ref[0, part]) + dot(low, table_ref[0, part]) + dot(high, table_ref[1, part])
        )
    for side, stress in enumerate((parts[0] + parts[1], parts[0] - parts[1])):
        first, second, third = stress[0:32], stress[32:64], stress[64:96]
        out_ref[:, side * HALF : (side + 1) * HALF] = jnp.sqrt(first * first + second * second + 1.0) + third


def spec(space=VMEM):
    return pl.BlockSpec(memory_space=space)


def run_forward(mask, slip, table, interpret=False):
    return pl.pallas_call(
        forward_rows,
        out_shape=jax.ShapeDtypeStruct((4 * DEVICES, 128), F32),
        in_specs=[spec()] * 3,
        out_specs=spec(),
        interpret=interpret,
        name="forward_rows",
    )(mask, slip, table)


def run_middle(position, slice_layer, layer_material, materials, table, twiddle, got, interpret=False):
    return pl.pallas_call(
        functools.partial(middle, position),
        out_shape=jax.ShapeDtypeStruct((3 * DEVICES, 128), F32),
        in_specs=[spec(SMEM)] * 3 + [spec()] * 3,
        out_specs=spec(),
        scratch_shapes=[
            VMEM((4, 384, 128), F32),
            VMEM((384, 512), F32),
            VMEM((R, 6, 4, 128), F32),
            VMEM((R, 8, 8, 128), F32),
            VMEM((4, 192, 128), F32),
        ],
        interpret=interpret,
        name="middle",
    )(slice_layer, layer_material, materials, table, twiddle, got)


def run_inverse(table, got, interpret=False):
    return pl.pallas_call(
        inverse_rows,
        out_shape=jax.ShapeDtypeStruct((32, GRID), F32),
        in_specs=[spec()] * 2,
        out_specs=spec(),
        interpret=interpret,
        name="inverse_rows",
    )(table, got)


def exchange(rows):
    blocks = rows.reshape((DEVICES, rows.shape[0] // DEVICES, 128))
    moved = lax.all_to_all(blocks, ("wave", "depth"), split_axis=0, concat_axis=0, tiled=True)
    return moved.reshape(rows.shape)


def shards(slip_field, slip_mask, slice_layer, layer_material, materials):
    real_dft, complex_dft, twiddle = tables()

    def position():
        return lax.axis_index("wave") * lax.axis_size("depth") + lax.axis_index("depth")

    sent = run_forward(slip_mask.reshape((2, 32)), slip_field.reshape((128, GRID)), real_dft)
    half = run_middle(
        position, slice_layer, layer_material, materials.reshape((24,)), complex_dft, twiddle, exchange(sent)
    )
    return run_inverse(real_dft, exchange(half)).reshape((1, 32, GRID))


def solution(mesh):
    placed = (P("depth", None, "wave", None), P("depth", "wave", None), P(), P(), P())
    return jax.shard_map(
        shards, mesh=mesh, in_specs=placed, out_specs=P("depth", "wave", None), check_vma=False
    )
```

```python
import functools
import math

import jax
import jax.numpy as jnp
import ml_dtypes
import numpy as np
from jax import lax
from jax.experimental import pallas as pl
from jax.experimental.pallas import tpu as pltpu
from jax.sharding import PartitionSpec as P

GRID = 1024
HALF = 512
QUARTER = 256
S = 16
R = 8
NZ = 64
DEVICES = 256
BF16 = jnp.bfloat16
F32 = jnp.float32
VMEM = pltpu.VMEM
SMEM = pltpu.SMEM


def split_table(table):
    high = table.astype(ml_dtypes.bfloat16)
    low = (table - high.astype(np.float64)).astype(ml_dtypes.bfloat16)
    return np.stack([high, low])


def tables():
    j = np.arange(QUARTER, dtype=np.int64)[:, None]
    cell = np.arange(HALF, dtype=np.int64)[None, :]
    rows = []
    for parity in range(2):
        angle = 2.0 * np.pi * (((2 * j + parity) * cell) % GRID) / GRID
        real, imag = np.cos(angle), -np.sin(angle)
        if parity == 0:
            imag[0] = 1.0 - 2.0 * (cell[0] % 2)
        rows += [real, imag]
    real_dft = np.concatenate(rows) / 32.0
    k = np.arange(QUARTER, dtype=np.int64)
    angle = 2.0 * np.pi * ((k[:, None] * k[None, :]) % QUARTER) / QUARTER
    cosine, sine = np.cos(angle) / 32.0, np.sin(angle) / 32.0
    complex_dft = np.block([[cosine, -sine], [sine, cosine]])
    turn = 2.0 * np.pi * np.arange(4)[:, None] * k[None, :] / GRID
    twiddle = np.concatenate([np.cos(turn), -np.sin(turn)]).astype(np.float32)
    return split_table(real_dft), split_table(complex_dft), twiddle


def halves(value):
    high = value.astype(BF16)
    return high, (value - high.astype(F32)).astype(BF16)


def dot(left, right, transposed=False):
    dims = (((1,), (1 if transposed else 0,)), ((), ()))
    return lax.dot_general(left, right, dims, preferred_element_type=F32)


def forward_rows(mask_ref, slip_ref, table_ref, out_ref):
    tile = lax.broadcasted_iota(jnp.int32, (32, GRID), 0)
    cell = lax.broadcasted_iota(jnp.int32, (32, GRID), 1)
    spread = (cell // 32 == tile).astype(BF16)
    mask = dot(mask_ref[...].astype(F32).astype(BF16), spread)
    slip = slip_ref[...].astype(F32)
    rows = slip.shape[0] // 2
    cells = jnp.concatenate([slip[:rows] * mask[0:1], slip[rows:] * mask[1:2]], axis=0)
    near, far = cells[:, :HALF], cells[:, HALF:]
    for parity, combined in enumerate((near + far, near - far)):
        high, low = halves(combined)
        part = slice(parity * HALF, (parity + 1) * HALF)
        result = (
            dot(table_ref[0, part], high, True)
            + dot(table_ref[0, part], low, True)
            + dot(table_ref[1, part], high, True)
        )
        for imag in range(2):
            out_ref[pl.ds(2 * parity + imag, QUARTER, stride=4), :] = result[
                imag * QUARTER : (imag + 1) * QUARTER
            ]


def swap_groups(items):
    lane = lax.broadcasted_iota(jnp.int32, items[0].shape, 1)
    for width in (2, 1):
        size = 32 * width
        upper = (lane // size) % 2 == 1
        out = list(items)
        for a in range(4):
            if a & width:
                continue
            b = a | width
            first, second = items[a], items[b]
            out[a] = jnp.where(upper, pltpu.roll(second, size, 1), first)
            out[b] = jnp.where(upper, second, pltpu.roll(first, 128 - size, 1))
        items = out
    return items


def radix_four(items):
    (r0, i0), (r1, i1), (r2, i2), (r3, i3) = items
    ar, ai, br, bi = r0 + r2, i0 + i2, r0 - r2, i0 - i2
    cr, ci, dr, di = r1 + r3, i1 + i3, r1 - r3, i1 - i3
    return [
        (ar + cr, ai + ci),
        (br + di, bi - dr),
        (ar - cr, ai - ci),
        (br - di, bi + dr),
    ]


def times(item, cosine, sine):
    real, imag = item
    return real * cosine - imag * sine, real * sine + imag * cosine


def depths(slice_ref, layer_ref, material_ref):
    center, rigidity, friction = [], [], []
    top = None
    for place in range(NZ):
        kind = layer_ref[slice_ref[place]]
        thickness = jnp.float32(0.1) * material_ref[kind]
        top = thickness if top is None else top + thickness
        center.append(top - 0.5 * thickness)
        if place % 8 == 3:
            rigidity.append(material_ref[8 + kind])
            friction.append(material_ref[16 + kind])
    source = [center[4 * s + 1] for s in range(S)]
    receiver = [center[8 * r + 3] for r in range(R)]
    return source, receiver, rigidity, friction


def geometry(first_row, rows, half, ky):
    k0 = lax.broadcasted_iota(jnp.int32, (rows, 128), 0) % 4
    k1 = lax.broadcasted_iota(jnp.int32, (rows, 128), 1) + 128 * half
    kx = 4 * k1 + k0
    signed = jnp.where(kx >= HALF, kx - GRID, kx)
    x_wave, y_wave = signed.astype(F32), ky.astype(F32)
    magnitude = jnp.sqrt(x_wave * x_wave + y_wave * y_wave)
    bounded = jnp.maximum(magnitude, 1.0)
    along_x, along_y = x_wave / bounded, y_wave / bounded
    x_edge, y_edge = signed == -HALF, ky == -HALF
    cross = jnp.where(x_edge != y_edge, 0.0, along_x * along_y)
    odd_x = jnp.where(x_edge, 0.0, along_x)
    odd_y = jnp.where(y_edge, 0.0, along_y)
    wave = 2.0 * math.pi / GRID * magnitude
    return wave, along_x * along_x, cross, along_y * along_y, odd_x, odd_y


def middle(
    j,
    columns,
    table_ref,
    twiddle_ref,
    got_ref,
    out_ref,
    left_ref,
    spec_ref,
    edge_ref,
    suffix_ref,
    trac_ref,
):
    first = j == 0
    source, receiver, rigidity, friction = columns
    keep_imag = jnp.where(first, 0.0, 1.0).astype(F32)
    only_first = 1.0 - keep_imag
    cosines = [twiddle_ref[a : a + 1, :] for a in range(4)]
    sines = [twiddle_ref[4 + a : 5 + a, :] for a in range(4)]

    loaded = [got_ref[pl.ds(c, DEVICES, stride=4), :] for c in range(4)]
    blocks = [[[None] * 8 for _ in range(4)] for _ in range(4)]
    for c in range(4):
        for outer in range(8):
            group = swap_groups([loaded[c][(4 * outer + inner) * 8 : (4 * outer + inner) * 8 + 8] for inner in range(4)])
            for g in range(4):
                blocks[c][g][outer] = group[g]
    for g in range(4):
        whole = [
            [jnp.concatenate([blocks[c][g][2 * x0], blocks[c][g][2 * x0 + 1]], axis=1) for x0 in range(4)]
            for c in range(4)
        ]
        kinds = [
            [(whole[0][x0], whole[1][x0] * keep_imag) for x0 in range(4)],
            [(whole[2][x0], whole[3][x0]) for x0 in range(4)],
            [(whole[1][x0], jnp.zeros_like(whole[1][x0])) for x0 in range(4)],
        ]
        for p in range(3):
            mixed = radix_four(kinds[p])
            for k0 in range(4):
                real, imag = times(mixed[k0], cosines[k0], sines[k0])
                if p < 2:
                    place = pl.ds(64 * g + 4 * p + k0, 8, stride=8)
                else:
                    place = pl.ds(256 + 32 * g + k0, 8, stride=4)
                for t in range(2):
                    left_ref.at[t][place, :] = real[:, 128 * t : 128 * t + 128]
                    left_ref.at[2 + t][place, :] = imag[:, 128 * t : 128 * t + 128]
    high, low = halves(jnp.concatenate([left_ref[t] for t in range(4)], axis=1))
    spectra = dot(high, table_ref[0]) + dot(low, table_ref[0]) + dot(high, table_ref[1])
    spec_ref[...] = spectra.astype(BF16).astype(F32)

    def unit(rows, base, step, half, ky, row_weight, write):
        wave, uu, uv, vv, odd_x, odd_y = geometry(0, rows, half, ky)

        def fields(s):
            picked = []
            for q in range(2):
                row = base + (2 * (s % 2) + q) * 8 * step + (s // 2) * step
                for imag in range(2):
                    start = 256 * imag + 128 * half
                    picked.append(spec_ref[row : row + rows, start : start + 128])
            return picked

        zero = jnp.zeros((rows, 128), F32)
        suffix, moment = [zero] * 4, [zero] * 4
        for s in reversed(range(S)):
            decay = jnp.exp(-wave * source[s])
            values = fields(s)
            scaled = [decay * value for value in values]
            suffix = [a + b for a, b in zip(suffix, scaled)]
            moment = [a + source[s] * b for a, b in zip(moment, scaled)]
            if s % 2 == 1:
                for n in range(4):
                    suffix_ref[s // 2, n, 0:rows, :] = suffix[n]
                    suffix_ref[s // 2, 4 + n, 0:rows, :] = moment[n]
        total, total_moment = suffix, moment
        prefix, moment = [zero] * 4, [zero] * 4
        for s in range(S - 1):
            growth = jnp.exp(wave * source[s])
            values = fields(s)
            scaled = [growth * value for value in values]
            prefix = [a + b for a, b in zip(prefix, scaled)]
            moment = [a + source[s] * b for a, b in zip(moment, scaled)]
            if s % 2 == 0:
                r = s // 2
                z = receiver[r]
                fall, rise = jnp.exp(-wave * z), jnp.exp(wave * z)
                summed, slope = [], []
                for n in range(4):
                    after, after_moment = suffix_ref[r, n, 0:rows, :], suffix_ref[r, 4 + n, 0:rows, :]
                    summed.append(fall * (prefix[n] + total[n]) + rise * after)
                    slope.append(
                        wave
                        * (
                            fall * (z * (prefix[n] - total[n]) - (moment[n] + total_moment[n]))
                            + rise * (after_moment - z * after)
                        )
                    )
                weight = row_weight * rigidity[r]
                along = [a - b for a, b in zip(summed, slope)]
                write(
                    r,
                    [
                        weight * (summed[0] - uu * slope[0] - uv * slope[2]),
                        weight * (summed[1] - uu * slope[1] - uv * slope[3]),
                        weight * (summed[2] - uv * slope[0] - vv * slope[2]),
                        weight * (summed[3] - uv * slope[1] - vv * slope[3]),
                        -weight * friction[r] * (odd_x * along[1] + odd_y * along[3]),
                        weight * friction[r] * (odd_x * along[0] + odd_y * along[2]),
                    ],
                )

    for half in range(2):

        def write_edge(r, values):
            for n in range(6):
                edge_ref[r, n] = values[n] * only_first

        unit(4, 256, 4, half, jnp.full((4, 128), -HALF, jnp.int32), jnp.ones((4, 128), F32), write_edge)

        def write_main(r, values):
            for c in range(3):
                real, imag = values[2 * c], values[2 * c + 1]
                pad = jnp.zeros((4, 128), F32)
                real = real - jnp.concatenate([edge_ref[r, 2 * c + 1], pad], axis=0)
                imag = imag + jnp.concatenate([edge_ref[r, 2 * c], pad], axis=0)
                place = pl.ds(64 * c + r, 8, stride=8)
                trac_ref.at[half][place, :] = real
                trac_ref.at[2 + half][place, :] = -imag

        kind = lax.broadcasted_iota(jnp.int32, (8, 128), 0) // 4
        weight = jnp.where(kind == 0, 1.0 + keep_imag, 2.0).astype(F32)
        unit(8, 0, 8, half, 2 * j + kind, weight, write_main)

    high, low = halves(jnp.concatenate([trac_ref[t] for t in range(4)], axis=1))
    turned = dot(high, table_ref[0]) + dot(low, table_ref[0]) + dot(high, table_ref[1])
    for c in range(3):
        fields = []
        for p in range(2):
            items = []
            for k0 in range(4):
                row = 64 * c + 32 * p + 8 * k0
                items.append(times((turned[row : row + 8, :256], turned[row : row + 8, 256:]), cosines[k0], sines[k0]))
            mixed = radix_four(items)
            fields.append([item[0] for item in mixed])
            fields.append([-item[1] for item in mixed])
        for outer in range(8):
            cut = slice(128 * (outer % 2), 128 * (outer % 2) + 128)
            group = swap_groups([fields[n][outer // 2][:, cut] for n in range(4)])
            for inner in range(4):
                w = 4 * outer + inner
                out_ref[pl.ds(32 * w + c, 8, stride=4), :] = group[inner]


def inverse_rows(table_ref, got_ref, out_ref):
    flipped = [got_ref[pl.ds(c, DEVICES, stride=4), :].T for c in range(3)]
    parts = []
    for parity in range(2):
        rows = []
        for c in range(3):
            real = flipped[c][64 * parity : 64 * parity + 32]
            imag = flipped[c][64 * parity + 32 : 64 * parity + 64]
            rows.append(jnp.concatenate([real, imag], axis=1))
        high, low = halves(jnp.concatenate(rows, axis=0))
        part = slice(parity * HALF, (parity + 1) * HALF)
        parts.append(
            dot(high, table_ref[0, part]) + dot(low, table_ref[0, part]) + dot(high, table_ref[1, part])
        )
    for side, stress in enumerate((parts[0] + parts[1], parts[0] - parts[1])):
        first, second, third = stress[0:32], stress[32:64], stress[64:96]
        out_ref[:, side * HALF : (side + 1) * HALF] = jnp.sqrt(first * first + second * second + 1.0) + third


NEAR = (4, 3, 5, 2, 6, 1, 7, 0)
MESH = pl.DeviceIdType.MESH


def fused(
    mask_ref,
    slip_ref,
    slice_ref,
    layer_ref,
    material_ref,
    twiddle_ref,
    real_hbm,
    complex_hbm,
    out_ref,
    real_ref,
    complex_ref,
    rows_ref,
    sent_ref,
    got_ref,
    send_ref,
    take_ref,
    left_ref,
    spec_ref,
    edge_ref,
    suffix_ref,
    trac_ref,
    table_sem,
    copy_sem,
    send_sem,
    take_sem,
    ready_sem,
):
    w, d = lax.axis_index("wave"), lax.axis_index("depth")
    me = w * 8 + d
    z, low, core = w // 4, (w // 2) % 2, w % 2
    high, y = d // 4, d % 4
    x = 2 * high + low
    rings = [((z + n) % 8) * 4 for n in range(8)]
    cores = [core, 1 - core]

    real_copy = pltpu.make_async_copy(real_hbm, real_ref, table_sem.at[0])
    complex_copy = pltpu.make_async_copy(complex_hbm, complex_ref, table_sem.at[1])
    real_copy.start()
    complex_copy.start()

    def greet(sem, pillar):
        for n in range(1, 16):
            if pillar:
                other = 2 * low if n < 8 else 2 - 2 * low
                place = (rings[n % 8] + other + core, d)
            else:
                side = 4 * high if (n // 2) % 2 == 0 else 4 - 4 * high
                place = (4 * z + 2 * low + cores[n % 2], side + (y + n // 4) % 4)
            pl.semaphore_signal(sem, 1, device_id=place, device_id_type=MESH)

    barrier = pltpu.get_barrier_semaphore()
    greet(barrier, True)
    greet(barrier, False)
    real_copy.wait()
    forward_rows(mask_ref, slip_ref, real_ref, rows_ref)
    sent_ref[...] = rows_ref[...].reshape(sent_ref.shape)
    pl.semaphore_wait(barrier, 30)
    greet(ready_sem, True)
    pl.semaphore_wait(ready_sem, 15)

    def exchange(source, target, number):
        def send(w_base, d_to, skip):
            for n in NEAR:
                for c in (1, 0):
                    if skip and n == 0 and c == 0:
                        continue
                    w_to = w_base + rings[n] + cores[c]
                    pltpu.make_async_remote_copy(
                        source.at[w_to * 8 + d_to],
                        target.at[me],
                        send_sem.at[number],
                        take_sem.at[number],
                        device_id=(w_to, d_to),
                        device_id_type=MESH,
                    ).start()

        def sheet(n, carry):
            order = (n + 11) % 16
            y_to, x_to = (y + order // 4 + 2) % 4, (x + order + 2) % 4
            send((x_to % 2) * 2, (x_to // 2) * 4 + y_to, False)
            return carry

        lax.fori_loop(0, 15, sheet, 0)
        send(2 * low, d, True)
        own = pltpu.make_async_copy(source.at[me], target.at[me], copy_sem.at[number])
        own.start()
        return own

    def finish(own, source, target, number):
        own.wait()
        most = pl.ds(0, DEVICES - 1)
        pltpu.make_async_copy(source.at[most], target.at[most], send_sem.at[number]).wait()
        pltpu.make_async_copy(source.at[most], target.at[most], take_sem.at[number]).wait()

    own = exchange(sent_ref, got_ref, 0)
    columns = depths(slice_ref, layer_ref, material_ref)
    complex_copy.wait()
    finish(own, sent_ref, got_ref, 0)
    rows_ref[...] = got_ref[...].reshape(rows_ref.shape)
    middle(
        me, columns, complex_ref, twiddle_ref, rows_ref, rows_ref, left_ref, spec_ref, edge_ref, suffix_ref, trac_ref
    )
    send_ref[...] = rows_ref[...].reshape(send_ref.shape).astype(BF16)
    own = exchange(send_ref, take_ref, 1)
    finish(own, send_ref, take_ref, 1)
    rows_ref[...] = take_ref[...].astype(F32).reshape(rows_ref.shape)
    inverse_rows(real_ref, rows_ref, out_ref)


def spec(space=VMEM):
    return pl.BlockSpec(memory_space=space)


def shards(slip_field, slip_mask, slice_layer, layer_material, materials):
    real_dft, complex_dft, twiddle = tables()
    result = pl.pallas_call(
        fused,
        out_shape=jax.ShapeDtypeStruct((32, GRID), F32),
        in_specs=[spec()] * 2 + [spec(SMEM)] * 3 + [spec()] + [spec(pl.ANY)] * 2,
        out_specs=spec(),
        scratch_shapes=[
            VMEM((2, GRID, HALF), BF16),
            VMEM((2, HALF, HALF), BF16),
            VMEM((4 * DEVICES, 128), F32),
            VMEM((DEVICES, 4, 128), F32),
            VMEM((DEVICES, 4, 128), F32),
            VMEM((DEVICES, 4, 128), BF16),
            VMEM((DEVICES, 4, 128), BF16),
            VMEM((4, 384, 128), F32),
            VMEM((384, 512), F32),
            VMEM((R, 6, 4, 128), F32),
            VMEM((R, 8, 8, 128), F32),
            VMEM((4, 192, 128), F32),
            pltpu.SemaphoreType.DMA((2,)),
            pltpu.SemaphoreType.DMA((2,)),
            pltpu.SemaphoreType.DMA((2,)),
            pltpu.SemaphoreType.DMA((2,)),
            pltpu.SemaphoreType.REGULAR,
        ],
        compiler_params=pltpu.CompilerParams(collective_id=0, has_side_effects=True),
        name="fused",
    )(
        slip_mask.reshape((2, 32)),
        slip_field.reshape((128, GRID)),
        slice_layer,
        layer_material,
        materials.reshape((24,)),
        twiddle,
        real_dft,
        complex_dft,
    )
    return result.reshape((1, 32, GRID))


def solution(mesh):
    placed = (P("depth", None, "wave", None), P("depth", "wave", None), P(), P(), P())
    return jax.shard_map(
        shards, mesh=mesh, in_specs=placed, out_specs=P("depth", "wave", None), check_vma=False
    )
```

```python
import functools
import math

import jax
import jax.numpy as jnp
import ml_dtypes
import numpy as np
from jax import lax
from jax.experimental import pallas as pl
from jax.experimental.pallas import tpu as pltpu
from jax.sharding import PartitionSpec as P

GRID = 1024
HALF = 512
QUARTER = 256
S = 16
R = 8
NZ = 64
DEVICES = 256
LARGEST = 6.0 * GRID / 32.0
CODE_SCALE = 32700.0 / LARGEST**0.25
BF16 = jnp.bfloat16
F32 = jnp.float32
VMEM = pltpu.VMEM
SMEM = pltpu.SMEM


def split_table(table):
    high = table.astype(ml_dtypes.bfloat16)
    low = (table - high.astype(np.float64)).astype(ml_dtypes.bfloat16)
    return np.stack([high, low])


def tables():
    j = np.arange(QUARTER, dtype=np.int64)[:, None]
    cell = np.arange(HALF, dtype=np.int64)[None, :]
    rows = []
    for parity in range(2):
        angle = 2.0 * np.pi * (((2 * j + parity) * cell) % GRID) / GRID
        real, imag = np.cos(angle), -np.sin(angle)
        if parity == 0:
            imag[0] = 1.0 - 2.0 * (cell[0] % 2)
        rows += [real, imag]
    real_dft = np.concatenate(rows) / 32.0
    k = np.arange(QUARTER, dtype=np.int64)
    angle = 2.0 * np.pi * ((k[:, None] * k[None, :]) % QUARTER) / QUARTER
    cosine, sine = np.cos(angle) / 32.0, np.sin(angle) / 32.0
    complex_dft = np.block([[cosine, -sine], [sine, cosine]])
    turn = 2.0 * np.pi * np.arange(4)[:, None] * k[None, :] / GRID
    twiddle = np.concatenate([np.cos(turn), -np.sin(turn)]).astype(np.float32)
    return split_table(real_dft), split_table(complex_dft), twiddle


def halves(value):
    high = value.astype(BF16)
    return high, (value - high.astype(F32)).astype(BF16)


def dot(left, right, transposed=False):
    dims = (((1,), (1 if transposed else 0,)), ((), ()))
    return lax.dot_general(left, right, dims, preferred_element_type=F32)


def forward_rows(mask_ref, slip_ref, table_ref, out_ref):
    tile = lax.broadcasted_iota(jnp.int32, (32, GRID), 0)
    cell = lax.broadcasted_iota(jnp.int32, (32, GRID), 1)
    spread = (cell // 32 == tile).astype(BF16)
    mask = dot(mask_ref[...].astype(F32).astype(BF16), spread)
    slip = slip_ref[...].astype(F32)
    rows = slip.shape[0] // 2
    cells = jnp.concatenate([slip[:rows] * mask[0:1], slip[rows:] * mask[1:2]], axis=0)
    near, far = cells[:, :HALF], cells[:, HALF:]
    for parity, combined in enumerate((near + far, near - far)):
        high, low = halves(combined)
        part = slice(parity * HALF, (parity + 1) * HALF)
        result = (
            dot(table_ref[0, part], high, True)
            + dot(table_ref[0, part], low, True)
            + dot(table_ref[1, part], high, True)
        )
        for imag in range(2):
            out_ref[pl.ds(2 * parity + imag, QUARTER, stride=4), :] = encode(
                result[imag * QUARTER : (imag + 1) * QUARTER]
            )


def swap_groups(items):
    lane = lax.broadcasted_iota(jnp.int32, items[0].shape, 1)
    for width in (2, 1):
        size = 32 * width
        upper = (lane // size) % 2 == 1
        out = list(items)
        for a in range(4):
            if a & width:
                continue
            b = a | width
            first, second = items[a], items[b]
            out[a] = jnp.where(upper, pltpu.roll(second, size, 1), first)
            out[b] = jnp.where(upper, second, pltpu.roll(first, 128 - size, 1))
        items = out
    return items


def encode(value):
    code = jnp.sqrt(jnp.sqrt(jnp.abs(value))) * CODE_SCALE + 0.5
    return jnp.where(value < 0.0, -code, code)


def decode(code):
    return (code * jnp.abs(code)) * (code * code) * (1.0 / CODE_SCALE) ** 4


def radix_four(items):
    (r0, i0), (r1, i1), (r2, i2), (r3, i3) = items
    ar, ai, br, bi = r0 + r2, i0 + i2, r0 - r2, i0 - i2
    cr, ci, dr, di = r1 + r3, i1 + i3, r1 - r3, i1 - i3
    return [
        (ar + cr, ai + ci),
        (br + di, bi - dr),
        (ar - cr, ai - ci),
        (br - di, bi + dr),
    ]


def times(item, cosine, sine):
    real, imag = item
    return real * cosine - imag * sine, real * sine + imag * cosine


def depths(slice_ref, layer_ref, material_ref):
    center, rigidity, friction = [], [], []
    top = None
    for place in range(NZ):
        kind = layer_ref[slice_ref[place]]
        thickness = jnp.float32(0.1) * material_ref[0, kind]
        top = thickness if top is None else top + thickness
        center.append(top - 0.5 * thickness)
        if place % 8 == 3:
            rigidity.append(material_ref[1, kind])
            friction.append(material_ref[2, kind])
    source = [center[4 * s + 1] for s in range(S)]
    receiver = [center[8 * r + 3] for r in range(R)]
    return source, receiver, rigidity, friction


def wave_arrays(sort, j):
    row = lax.broadcasted_iota(jnp.int32, (8, 128), 0)
    lane = lax.broadcasted_iota(jnp.int32, (8, 128), 1)
    half = row // 4 if sort == 2 else sort
    kx = 4 * (lane + 128 * half) + row % 4
    signed = jnp.where(kx >= HALF, kx - GRID, kx)
    ky = jnp.full((8, 128), -HALF, jnp.int32) if sort == 2 else 2 * j + row // 4
    x_wave, y_wave = signed.astype(F32), ky.astype(F32)
    magnitude = jnp.sqrt(x_wave * x_wave + y_wave * y_wave)
    bounded = jnp.maximum(magnitude, 1.0)
    along_x, along_y = x_wave / bounded, y_wave / bounded
    x_edge = signed == -HALF
    y_edge = ky == -HALF
    cross = jnp.where(x_edge != y_edge, 0.0, along_x * along_y)
    odd_x = jnp.where(x_edge, 0.0, along_x)
    odd_y = jnp.where(y_edge, 0.0, along_y)
    wave = 2.0 * math.pi / GRID * magnitude
    return wave, along_x * along_x, cross, along_y * along_y, odd_x, odd_y


def prepare(j, columns, wave_ref, grow_ref, fall_ref):
    source, receiver = columns[0], columns[1]
    for sort in range(3):
        arrays = wave_arrays(sort, j)
        for n, value in enumerate(arrays):
            wave_ref[sort, n] = value
        for n, z in enumerate(source + receiver):
            exponent = arrays[0] * z
            grow_ref[sort, n] = jnp.exp(exponent)
            fall_ref[sort, n] = jnp.exp(-exponent)


def middle(
    j,
    columns,
    table_ref,
    twiddle_ref,
    got_ref,
    out_ref,
    left_ref,
    spec_ref,
    rim_ref,
    edge_ref,
    suffix_ref,
    trac_ref,
    wave_ref,
    grow_ref,
    fall_ref,
):
    source, receiver, rigidity, friction = columns
    keep_imag = jnp.where(j == 0, 0.0, 1.0).astype(F32)
    only_first = 1.0 - keep_imag
    cosines = [twiddle_ref[a : a + 1, :] for a in range(4)]
    sines = [twiddle_ref[4 + a : 5 + a, :] for a in range(4)]

    loaded = [decode(got_ref[pl.ds(c, DEVICES, stride=4), :]) for c in range(4)]
    blocks = [[[None] * 8 for _ in range(4)] for _ in range(4)]
    for c in range(4):
        for outer in range(8):
            group = swap_groups([loaded[c][(4 * outer + inner) * 8 : (4 * outer + inner) * 8 + 8] for inner in range(4)])
            for g in range(4):
                blocks[c][g][outer] = group[g]
    for g in range(4):
        whole = [
            [jnp.concatenate([blocks[c][g][2 * x0], blocks[c][g][2 * x0 + 1]], axis=1) for x0 in range(4)]
            for c in range(4)
        ]
        kinds = [
            [(whole[0][x0], whole[1][x0] * keep_imag) for x0 in range(4)],
            [(whole[2][x0], whole[3][x0]) for x0 in range(4)],
            [(whole[1][x0], jnp.zeros_like(whole[1][x0])) for x0 in range(4)],
        ]
        for p in range(3):
            mixed = radix_four(kinds[p])
            for k0 in range(4):
                real, imag = times(mixed[k0], cosines[k0], sines[k0]) if k0 else mixed[k0]
                if p < 2:
                    place = pl.ds(64 * g + 4 * p + k0, 8, stride=8)
                else:
                    place = pl.ds(256 + 32 * k0 + 8 * g, 8)
                for t in range(2):
                    left_ref.at[t][place, :] = real[:, 128 * t : 128 * t + 128]
                    left_ref.at[2 + t][place, :] = imag[:, 128 * t : 128 * t + 128]
    high, low = halves(jnp.concatenate([left_ref[t] for t in range(4)], axis=1))
    spectra = dot(high, table_ref[0]) + dot(low, table_ref[0]) + dot(high, table_ref[1])
    spectra = spectra.astype(BF16).astype(F32)
    spec_ref[...] = spectra[:256]
    for k0 in range(4):
        for t in range(4):
            rows = spectra[256 + 32 * k0 : 288 + 32 * k0, 128 * t : 128 * t + 128]
            rim_ref.at[t // 2][pl.ds(4 * (t % 2) + k0, 32, stride=8), :] = rows

    def unit(sort, row_weight, write):
        wave, uu, uv, vv, odd_x, odd_y = [wave_ref[sort, n] for n in range(6)]

        def fields(s):
            picked = []
            for q in range(2):
                row = 8 * ((2 * (s % 2) + q) * 8 + s // 2)
                for imag in range(2):
                    if sort == 2:
                        picked.append(rim_ref[imag, row : row + 8, :])
                    else:
                        start = 256 * imag + 128 * sort
                        picked.append(spec_ref[row : row + 8, start : start + 128])
            return picked

        zero = jnp.zeros((8, 128), F32)
        suffix, moment = [zero] * 4, [zero] * 4
        for s in reversed(range(S)):
            decay = fall_ref[sort, s]
            scaled = [decay * value for value in fields(s)]
            suffix = [a + b for a, b in zip(suffix, scaled)]
            moment = [a + source[s] * b for a, b in zip(moment, scaled)]
            if s % 2 == 1:
                for n in range(4):
                    suffix_ref[s // 2, n] = suffix[n]
                    suffix_ref[s // 2, 4 + n] = moment[n]
        total, total_moment = suffix, moment
        prefix, moment = [zero] * 4, [zero] * 4
        for s in range(S - 1):
            growth = grow_ref[sort, s]
            scaled = [growth * value for value in fields(s)]
            prefix = [a + b for a, b in zip(prefix, scaled)]
            moment = [a + source[s] * b for a, b in zip(moment, scaled)]
            if s % 2 == 0:
                r = s // 2
                z = receiver[r]
                fall, rise = fall_ref[sort, S + r], grow_ref[sort, S + r]
                wave_fall, wave_rise = wave * fall, wave * rise
                summed, slope = [], []
                for n in range(4):
                    after, after_moment = suffix_ref[r, n], suffix_ref[r, 4 + n]
                    summed.append(fall * (prefix[n] + total[n]) + rise * after)
                    slope.append(
                        wave_fall * (z * (prefix[n] - total[n]) - (moment[n] + total_moment[n]))
                        + wave_rise * (after_moment - z * after)
                    )
                weight = row_weight * rigidity[r]
                tilt = weight * friction[r]
                along = [a - b for a, b in zip(summed, slope)]
                write(
                    r,
                    [
                        weight * (summed[0] - uu * slope[0] - uv * slope[2]),
                        weight * (summed[1] - uu * slope[1] - uv * slope[3]),
                        weight * (summed[2] - uv * slope[0] - vv * slope[2]),
                        weight * (summed[3] - uv * slope[1] - vv * slope[3]),
                        -tilt * (odd_x * along[1] + odd_y * along[3]),
                        tilt * (odd_x * along[0] + odd_y * along[2]),
                    ],
                )

    def write_edge(r, values):
        for n in range(6):
            edge_ref[r, n] = values[n]

    unit(2, only_first, write_edge)
    kind = lax.broadcasted_iota(jnp.int32, (8, 128), 0) // 4
    weight = jnp.where(kind == 0, 1.0 + keep_imag, 2.0).astype(F32)
    pad = jnp.zeros((4, 128), F32)
    for half in range(2):

        def write_main(r, values):
            for c in range(3):
                edges = [
                    jnp.concatenate([edge_ref[r, 2 * c + n, 4 * half : 4 * half + 4, :], pad], axis=0) for n in range(2)
                ]
                place = pl.ds(64 * c + r, 8, stride=8)
                trac_ref.at[half][place, :] = values[2 * c] - edges[1]
                trac_ref.at[2 + half][place, :] = -(values[2 * c + 1] + edges[0])

        unit(half, weight, write_main)

    high, low = halves(jnp.concatenate([trac_ref[t] for t in range(4)], axis=1))
    turned = dot(high, table_ref[0]) + dot(low, table_ref[0]) + dot(high, table_ref[1])
    for c in range(3):
        fields = []
        for p in range(2):
            items = []
            for k0 in range(4):
                row = 64 * c + 32 * p + 8 * k0
                item = (turned[row : row + 8, :256], turned[row : row + 8, 256:])
                items.append(times(item, cosines[k0], sines[k0]) if k0 else item)
            mixed = radix_four(items)
            fields.append([item[0] for item in mixed])
            fields.append([-item[1] for item in mixed])
        for outer in range(8):
            cut = slice(128 * (outer % 2), 128 * (outer % 2) + 128)
            group = swap_groups([fields[n][outer // 2][:, cut] for n in range(4)])
            for inner in range(4):
                w = 4 * outer + inner
                out_ref[pl.ds(32 * w + c, 8, stride=4), :] = group[inner]


def inverse_rows(table_ref, got_ref, out_ref):
    flipped = [got_ref[pl.ds(c, DEVICES, stride=4), :].T for c in range(3)]
    parts = []
    for parity in range(2):
        rows = []
        for c in range(3):
            real = flipped[c][64 * parity : 64 * parity + 32]
            imag = flipped[c][64 * parity + 32 : 64 * parity + 64]
            rows.append(jnp.concatenate([real, imag], axis=1))
        whole = jnp.concatenate(rows, axis=0).astype(BF16)
        part = slice(parity * HALF, (parity + 1) * HALF)
        parts.append(dot(whole, table_ref[0, part]) + dot(whole, table_ref[1, part]))
    for side, stress in enumerate((parts[0] + parts[1], parts[0] - parts[1])):
        first, second, third = stress[0:32], stress[32:64], stress[64:96]
        out_ref[:, side * HALF : (side + 1) * HALF] = jnp.sqrt(first * first + second * second + 1.0) + third


NEAR = (4, 3, 5, 2, 6, 1, 7, 0)
MESH = pl.DeviceIdType.MESH


def fused(
    mask_hbm,
    slip_hbm,
    slice_hbm,
    layer_hbm,
    material_hbm,
    twiddle_hbm,
    real_hbm,
    complex_hbm,
    out_ref,
    mask_ref,
    slip_ref,
    slice_ref,
    layer_ref,
    material_ref,
    twiddle_ref,
    real_ref,
    complex_ref,
    rows_ref,
    sent_ref,
    got_ref,
    send_ref,
    take_ref,
    left_ref,
    spec_ref,
    rim_ref,
    edge_ref,
    suffix_ref,
    trac_ref,
    wave_ref,
    grow_ref,
    fall_ref,
    input_sem,
    copy_sem,
    send_sem,
    take_sem,
    ready_sem,
):
    w, d = lax.axis_index("wave"), lax.axis_index("depth")
    me = w * 8 + d
    z, low, core = w // 4, (w // 2) % 2, w % 2
    high, y = d // 4, d % 4
    x = 2 * high + low
    rings = [((z + n) % 8) * 4 for n in range(8)]
    cores = [core, 1 - core]

    def greet(sem, pillar):
        for n in range(1, 16):
            if pillar:
                other = 2 * low if n < 8 else 2 - 2 * low
                place = (rings[n % 8] + other + core, d)
            else:
                side = 4 * high if (n // 2) % 2 == 0 else 4 - 4 * high
                place = (4 * z + 2 * low + cores[n % 2], side + (y + n // 4) % 4)
            pl.semaphore_signal(sem, 1, device_id=place, device_id_type=MESH)

    barrier = pltpu.get_barrier_semaphore()
    greet(barrier, True)
    greet(barrier, False)
    pairs = (
        (slip_hbm, slip_ref),
        (mask_hbm, mask_ref),
        (real_hbm, real_ref),
        (slice_hbm, slice_ref),
        (layer_hbm, layer_ref),
        (material_hbm, material_ref),
        (twiddle_hbm, twiddle_ref),
        (complex_hbm, complex_ref),
    )
    copies = [pltpu.make_async_copy(a, b, input_sem.at[n]) for n, (a, b) in enumerate(pairs)]
    for copy in copies:
        copy.start()
    for copy in copies[:3]:
        copy.wait()
    forward_rows(mask_ref, slip_ref, real_ref, rows_ref)
    sent_ref[...] = rows_ref[...].reshape(sent_ref.shape).astype(jnp.int32).astype(jnp.int16)
    pl.semaphore_wait(barrier, 30)
    greet(ready_sem, True)
    pl.semaphore_wait(ready_sem, 15)

    def exchange(source, target, number):
        def send(w_base, d_to, skip):
            for n in NEAR:
                for c in (1, 0):
                    if skip and n == 0 and c == 0:
                        continue
                    w_to = w_base + rings[n] + cores[c]
                    pltpu.make_async_remote_copy(
                        source.at[w_to * 8 + d_to],
                        target.at[me],
                        send_sem.at[number],
                        take_sem.at[number],
                        device_id=(w_to, d_to),
                        device_id_type=MESH,
                    ).start()

        def sheet(n, carry):
            order = (n + 11) % 16
            y_to, x_to = (y + order // 4 + 2) % 4, (x + order + 2) % 4
            send((x_to % 2) * 2, (x_to // 2) * 4 + y_to, False)
            return carry

        lax.fori_loop(0, 15, sheet, 0)
        send(2 * low, d, True)
        own = pltpu.make_async_copy(source.at[me], target.at[me], copy_sem.at[number])
        own.start()
        return own

    def finish(own, source, target, number):
        own.wait()
        most = pl.ds(0, DEVICES - 1)
        pltpu.make_async_copy(source.at[most], target.at[most], send_sem.at[number]).wait()
        pltpu.make_async_copy(source.at[most], target.at[most], take_sem.at[number]).wait()

    own = exchange(sent_ref, got_ref, 0)
    for copy in copies[3:]:
        copy.wait()
    columns = depths(slice_ref, layer_ref, material_ref)
    prepare(me, columns, wave_ref, grow_ref, fall_ref)
    finish(own, sent_ref, got_ref, 0)
    rows_ref[...] = got_ref[...].astype(jnp.int32).astype(F32).reshape(rows_ref.shape)
    middle(
        me,
        columns,
        complex_ref,
        twiddle_ref,
        rows_ref,
        rows_ref,
        left_ref,
        spec_ref,
        rim_ref,
        edge_ref,
        suffix_ref,
        trac_ref,
        wave_ref,
        grow_ref,
        fall_ref,
    )
    send_ref[...] = rows_ref[...].reshape(send_ref.shape).astype(BF16)
    own = exchange(send_ref, take_ref, 1)
    finish(own, send_ref, take_ref, 1)
    rows_ref[...] = take_ref[...].astype(F32).reshape(rows_ref.shape)
    inverse_rows(real_ref, rows_ref, out_ref)


def spec(space=VMEM):
    return pl.BlockSpec(memory_space=space)


def shards(slip_field, slip_mask, slice_layer, layer_material, materials):
    real_dft, complex_dft, twiddle = tables()
    result = pl.pallas_call(
        fused,
        out_shape=jax.ShapeDtypeStruct((32, GRID), F32),
        in_specs=[spec(pl.ANY)] * 8,
        out_specs=spec(),
        scratch_shapes=[
            VMEM((2, 32), jnp.int32),
            VMEM((128, GRID), BF16),
            SMEM((NZ,), jnp.int32),
            SMEM((16,), jnp.int32),
            SMEM((3, 8), F32),
            VMEM((8, QUARTER), F32),
            VMEM((2, GRID, HALF), BF16),
            VMEM((2, HALF, HALF), BF16),
            VMEM((4 * DEVICES, 128), F32),
            VMEM((DEVICES, 4, 128), jnp.int16),
            VMEM((DEVICES, 4, 128), jnp.int16),
            VMEM((DEVICES, 4, 128), BF16),
            VMEM((DEVICES, 4, 128), BF16),
            VMEM((4, 384, 128), F32),
            VMEM((256, 512), F32),
            VMEM((2, 256, 128), F32),
            VMEM((R, 6, 8, 128), F32),
            VMEM((R, 8, 8, 128), F32),
            VMEM((4, 192, 128), F32),
            VMEM((3, 6, 8, 128), F32),
            VMEM((3, S + R, 8, 128), F32),
            VMEM((3, S + R, 8, 128), F32),
            pltpu.SemaphoreType.DMA((8,)),
            pltpu.SemaphoreType.DMA((2,)),
            pltpu.SemaphoreType.DMA((2,)),
            pltpu.SemaphoreType.DMA((2,)),
            pltpu.SemaphoreType.REGULAR,
        ],
        compiler_params=pltpu.CompilerParams(collective_id=0, has_side_effects=True),
        name="fused",
    )(
        slip_mask.reshape((2, 32)),
        slip_field.reshape((128, GRID)),
        slice_layer,
        layer_material,
        materials,
        twiddle,
        real_dft,
        complex_dft,
    )
    return result.reshape((1, 32, GRID))


def solution(mesh):
    placed = (P("depth", None, "wave", None), P("depth", "wave", None), P(), P(), P())
    return jax.shard_map(
        shards, mesh=mesh, in_specs=placed, out_specs=P("depth", "wave", None), check_vma=False
    )
```

```python
import functools
import math

import jax
import jax.numpy as jnp
import ml_dtypes
import numpy as np
from jax import lax
from jax.experimental import pallas as pl
from jax.experimental.pallas import tpu as pltpu
from jax.sharding import PartitionSpec as P

GRID = 1024
HALF = 512
QUARTER = 256
S = 16
R = 8
NZ = 64
DEVICES = 256
LARGEST = 6.0 * GRID / 32.0
CODE_SCALE = 32700.0 / LARGEST**0.25
BF16 = jnp.bfloat16
F32 = jnp.float32
VMEM = pltpu.VMEM
SMEM = pltpu.SMEM


def split_table(table):
    high = table.astype(ml_dtypes.bfloat16)
    low = (table - high.astype(np.float64)).astype(ml_dtypes.bfloat16)
    return np.stack([high, low])


def tables():
    j = np.arange(QUARTER, dtype=np.int64)[:, None]
    cell = np.arange(HALF, dtype=np.int64)[None, :]
    rows = []
    for parity in range(2):
        angle = 2.0 * np.pi * (((2 * j + parity) * cell) % GRID) / GRID
        real, imag = np.cos(angle), -np.sin(angle)
        if parity == 0:
            imag[0] = 1.0 - 2.0 * (cell[0] % 2)
        rows += [real, imag]
    real_dft = np.concatenate(rows) / 32.0
    k = np.arange(128, dtype=np.int64)
    angle = 2.0 * np.pi * ((k[:, None] * k[None, :]) % 128) / 128
    cosine, sine = np.cos(angle) / 32.0, np.sin(angle) / 32.0
    complex_dft = np.block([[cosine, -sine], [sine, cosine]])
    turn = 2.0 * np.pi * np.arange(8)[:, None] * k[None, :] / GRID
    twiddle = np.concatenate([np.cos(turn), -np.sin(turn)]).astype(np.float32)
    return split_table(real_dft), split_table(complex_dft), twiddle


def halves(value):
    high = value.astype(BF16)
    return high, (value - high.astype(F32)).astype(BF16)


def dot(left, right, transposed=False):
    dims = (((1,), (1 if transposed else 0,)), ((), ()))
    return lax.dot_general(left, right, dims, preferred_element_type=F32)


def forward_rows(mask_ref, slip_ref, table_ref, out_ref):
    tile = lax.broadcasted_iota(jnp.int32, (32, GRID), 0)
    cell = lax.broadcasted_iota(jnp.int32, (32, GRID), 1)
    spread = (cell // 32 == tile).astype(BF16)
    mask = dot(mask_ref[...].astype(F32).astype(BF16), spread)
    slip = slip_ref[...].astype(F32)
    rows = slip.shape[0] // 2
    cells = jnp.concatenate([slip[:rows] * mask[0:1], slip[rows:] * mask[1:2]], axis=0)
    near, far = cells[:, :HALF], cells[:, HALF:]
    for parity, combined in enumerate((near + far, near - far)):
        high, low = halves(combined)
        part = slice(parity * HALF, (parity + 1) * HALF)
        result = (
            dot(table_ref[0, part], high, True)
            + dot(table_ref[0, part], low, True)
            + dot(table_ref[1, part], high, True)
        )
        for imag in range(2):
            out_ref[pl.ds(2 * parity + imag, QUARTER, stride=4), :] = encode(
                result[imag * QUARTER : (imag + 1) * QUARTER]
            )


def swap_groups(items):
    lane = lax.broadcasted_iota(jnp.int32, items[0].shape, 1)
    for width in (2, 1):
        size = 32 * width
        upper = (lane // size) % 2 == 1
        out = list(items)
        for a in range(4):
            if a & width:
                continue
            b = a | width
            first, second = items[a], items[b]
            out[a] = jnp.where(upper, pltpu.roll(second, size, 1), first)
            out[b] = jnp.where(upper, second, pltpu.roll(first, 128 - size, 1))
        items = out
    return items


def encode(value):
    code = jnp.sqrt(jnp.sqrt(jnp.abs(value))) * CODE_SCALE + 0.5
    return jnp.where(value < 0.0, -code, code)


def decode(code):
    return (code * jnp.abs(code)) * (code * code) * (1.0 / CODE_SCALE) ** 4


def radix_four(items):
    (r0, i0), (r1, i1), (r2, i2), (r3, i3) = items
    ar, ai, br, bi = r0 + r2, i0 + i2, r0 - r2, i0 - i2
    cr, ci, dr, di = r1 + r3, i1 + i3, r1 - r3, i1 - i3
    return [
        (ar + cr, ai + ci),
        (br + di, bi - dr),
        (ar - cr, ai - ci),
        (br - di, bi + dr),
    ]


def radix_eight(items):
    even, odd = radix_four(items[0::2]), radix_four(items[1::2])
    root = math.sqrt(0.5)
    (r0, i0), (r1, i1), (r2, i2), (r3, i3) = odd
    turned = [(r0, i0), (root * (r1 + i1), root * (i1 - r1)), (i2, -r2), (root * (i3 - r3), -root * (r3 + i3))]
    return [(a[0] + b[0], a[1] + b[1]) for a, b in zip(even, turned)] + [
        (a[0] - b[0], a[1] - b[1]) for a, b in zip(even, turned)
    ]


def times(item, cosine, sine):
    real, imag = item
    return real * cosine - imag * sine, real * sine + imag * cosine


def depths(slice_ref, layer_ref, material_ref):
    center, rigidity, friction = [], [], []
    top = None
    for place in range(NZ):
        kind = layer_ref[slice_ref[place]]
        thickness = jnp.float32(0.1) * material_ref[0, kind]
        top = thickness if top is None else top + thickness
        center.append(top - 0.5 * thickness)
        if place % 8 == 3:
            rigidity.append(material_ref[1, kind])
            friction.append(material_ref[2, kind])
    source = [center[4 * s + 1] for s in range(S)]
    receiver = [center[8 * r + 3] for r in range(R)]
    return source, receiver, rigidity, friction


def wave_arrays(kind, j):
    kx = 8 * lax.broadcasted_iota(jnp.int32, (8, 128), 1) + lax.broadcasted_iota(jnp.int32, (8, 128), 0)
    signed = jnp.where(kx >= HALF, kx - GRID, kx)
    ky = jnp.full((8, 128), -HALF, jnp.int32) if kind == 2 else jnp.full((8, 128), 2 * j + kind, jnp.int32)
    x_wave, y_wave = signed.astype(F32), ky.astype(F32)
    magnitude = jnp.sqrt(x_wave * x_wave + y_wave * y_wave)
    bounded = jnp.maximum(magnitude, 1.0)
    along_x, along_y = x_wave / bounded, y_wave / bounded
    x_edge = signed == -HALF
    y_edge = ky == -HALF
    cross = jnp.where(x_edge != y_edge, 0.0, along_x * along_y)
    odd_x = jnp.where(x_edge, 0.0, along_x)
    odd_y = jnp.where(y_edge, 0.0, along_y)
    wave = 2.0 * math.pi / GRID * magnitude
    return wave, along_x * along_x, cross, along_y * along_y, odd_x, odd_y


def prepare(j, columns, wave_ref, grow_ref, fall_ref):
    source, receiver = columns[0], columns[1]
    for kind in range(3):
        arrays = wave_arrays(kind, j)
        for n, value in enumerate(arrays):
            wave_ref[kind, n] = value
        for n, z in enumerate(source + receiver):
            exponent = arrays[0] * z
            grow_ref[kind, n] = jnp.exp(exponent)
            fall_ref[kind, n] = jnp.exp(-exponent)


def middle(
    j,
    columns,
    table_ref,
    twiddle_ref,
    got_ref,
    out_ref,
    left_ref,
    spec_ref,
    edge_ref,
    suffix_ref,
    trac_ref,
    wave_ref,
    grow_ref,
    fall_ref,
):
    source, receiver, rigidity, friction = columns
    keep_imag = jnp.where(j == 0, 0.0, 1.0).astype(F32)
    only_first = 1.0 - keep_imag
    cosines = [twiddle_ref[a : a + 1, :] for a in range(8)]
    sines = [twiddle_ref[8 + a : 9 + a, :] for a in range(8)]

    loaded = [decode(got_ref[pl.ds(c, DEVICES, stride=4), :]) for c in range(4)]
    blocks = [[[None] * 8 for _ in range(4)] for _ in range(4)]
    for c in range(4):
        for outer in range(8):
            group = swap_groups([loaded[c][(4 * outer + inner) * 8 : (4 * outer + inner) * 8 + 8] for inner in range(4)])
            for g in range(4):
                blocks[c][g][outer] = group[g]
    for g in range(4):
        kinds = [
            [(blocks[0][g][o], blocks[1][g][o] * keep_imag) for o in range(8)],
            [(blocks[2][g][o], blocks[3][g][o]) for o in range(8)],
            [(blocks[1][g][o], jnp.zeros_like(blocks[1][g][o])) for o in range(8)],
        ]
        for kind in range(3):
            mixed = radix_eight(kinds[kind])
            for k0 in range(8):
                real, imag = times(mixed[k0], cosines[k0], sines[k0]) if k0 else mixed[k0]
                place = pl.ds(64 * (4 * kind + g) + k0, 8, stride=8)
                left_ref.at[0][place, :] = real
                left_ref.at[1][place, :] = imag
    high, low = halves(jnp.concatenate([left_ref[0], left_ref[1]], axis=1))
    spectra = dot(high, table_ref[0]) + dot(low, table_ref[0]) + dot(high, table_ref[1])
    spec_ref[...] = spectra.astype(BF16).astype(F32)

    def unit(kind, row_weight, write):
        wave, uu, uv, vv, odd_x, odd_y = [wave_ref[kind, n] for n in range(6)]

        def fields(s):
            rows = [8 * (8 * (4 * kind + 2 * (s % 2) + q) + s // 2) for q in range(2)]
            return [spec_ref[row : row + 8, 128 * n : 128 * n + 128] for row in rows for n in range(2)]

        zero = jnp.zeros((8, 128), F32)
        suffix, moment = [zero] * 4, [zero] * 4
        for s in reversed(range(S)):
            decay = fall_ref[kind, s]
            scaled = [decay * value for value in fields(s)]
            suffix = [a + b for a, b in zip(suffix, scaled)]
            moment = [a + source[s] * b for a, b in zip(moment, scaled)]
            if s % 2 == 1:
                for n in range(4):
                    suffix_ref[s // 2, n] = suffix[n]
                    suffix_ref[s // 2, 4 + n] = moment[n]
        total, total_moment = suffix, moment
        prefix, moment = [zero] * 4, [zero] * 4
        for s in range(S - 1):
            growth = grow_ref[kind, s]
            scaled = [growth * value for value in fields(s)]
            prefix = [a + b for a, b in zip(prefix, scaled)]
            moment = [a + source[s] * b for a, b in zip(moment, scaled)]
            if s % 2 == 0:
                r = s // 2
                z = receiver[r]
                fall, rise = fall_ref[kind, S + r], grow_ref[kind, S + r]
                wave_fall, wave_rise = wave * fall, wave * rise
                summed, slope = [], []
                for n in range(4):
                    after, after_moment = suffix_ref[r, n], suffix_ref[r, 4 + n]
                    summed.append(fall * (prefix[n] + total[n]) + rise * after)
                    slope.append(
                        wave_fall * (z * (prefix[n] - total[n]) - (moment[n] + total_moment[n]))
                        + wave_rise * (after_moment - z * after)
                    )
                weight = row_weight * rigidity[r]
                tilt = weight * friction[r]
                along = [a - b for a, b in zip(summed, slope)]
                write(
                    r,
                    [
                        weight * (summed[0] - uu * slope[0] - uv * slope[2]),
                        weight * (summed[1] - uu * slope[1] - uv * slope[3]),
                        weight * (summed[2] - uv * slope[0] - vv * slope[2]),
                        weight * (summed[3] - uv * slope[1] - vv * slope[3]),
                        -tilt * (odd_x * along[1] + odd_y * along[3]),
                        tilt * (odd_x * along[0] + odd_y * along[2]),
                    ],
                )

    def write_edge(r, values):
        for n in range(6):
            edge_ref[r, n] = values[n]

    unit(2, only_first, write_edge)
    for p in range(2):

        def write_main(r, values):
            for c in range(3):
                real, imag = values[2 * c], values[2 * c + 1]
                if p == 0:
                    real, imag = real - edge_ref[r, 2 * c + 1], imag + edge_ref[r, 2 * c]
                place = pl.ds(64 * (2 * c + p) + r, 8, stride=8)
                trac_ref.at[0][place, :] = real
                trac_ref.at[1][place, :] = -imag

        unit(p, jnp.float32(2.0) if p else 1.0 + keep_imag, write_main)

    high, low = halves(jnp.concatenate([trac_ref[0], trac_ref[1]], axis=1))
    turned = dot(high, table_ref[0]) + dot(low, table_ref[0]) + dot(high, table_ref[1])
    for c in range(3):
        fields = []
        for p in range(2):
            items = []
            for k0 in range(8):
                row = 64 * (2 * c + p) + 8 * k0
                item = (turned[row : row + 8, :128], turned[row : row + 8, 128:])
                items.append(times(item, cosines[k0], sines[k0]) if k0 else item)
            mixed = radix_eight(items)
            fields.append([item[0] for item in mixed])
            fields.append([-item[1] for item in mixed])
        for outer in range(8):
            group = swap_groups([fields[n][outer] for n in range(4)])
            for inner in range(4):
                w = 4 * outer + inner
                out_ref[pl.ds(32 * w + c, 8, stride=4), :] = group[inner]


def inverse_rows(table_ref, got_ref, out_ref):
    flipped = [got_ref[pl.ds(c, DEVICES, stride=4), :].T for c in range(3)]
    parts = []
    for parity in range(2):
        rows = []
        for c in range(3):
            real = flipped[c][64 * parity : 64 * parity + 32]
            imag = flipped[c][64 * parity + 32 : 64 * parity + 64]
            rows.append(jnp.concatenate([real, imag], axis=1))
        whole = jnp.concatenate(rows, axis=0).astype(BF16)
        part = slice(parity * HALF, (parity + 1) * HALF)
        parts.append(dot(whole, table_ref[0, part]) + dot(whole, table_ref[1, part]))
    for side, stress in enumerate((parts[0] + parts[1], parts[0] - parts[1])):
        first, second, third = stress[0:32], stress[32:64], stress[64:96]
        out_ref[:, side * HALF : (side + 1) * HALF] = jnp.sqrt(first * first + second * second + 1.0) + third


MESH = pl.DeviceIdType.MESH


def far_first():
    places = [(z, y, x, c) for z in range(8) for y in range(4) for x in range(4) for c in range(2)][1:]

    def rank(place):
        z, y, x, c = place
        hops = min(z, 8 - z) + min(y, 4 - y) + min(x, 4 - x)
        return -hops, (z * 89 + y * 37 + x * 53 + c * 101) % 61, place

    return sorted(places, key=rank)


def fused(
    mask_hbm,
    slip_hbm,
    slice_hbm,
    layer_hbm,
    material_hbm,
    twiddle_hbm,
    real_hbm,
    complex_hbm,
    out_ref,
    mask_ref,
    slip_ref,
    slice_ref,
    layer_ref,
    material_ref,
    twiddle_ref,
    real_ref,
    complex_ref,
    rows_ref,
    sent_ref,
    got_ref,
    send_ref,
    take_ref,
    left_ref,
    spec_ref,
    edge_ref,
    suffix_ref,
    trac_ref,
    wave_ref,
    grow_ref,
    fall_ref,
    input_sem,
    copy_sem,
    send_sem,
    take_sem,
):
    w, d = lax.axis_index("wave"), lax.axis_index("depth")
    me = w * 8 + d
    z, low, core = w // 4, (w // 2) % 2, w % 2
    high, y = d // 4, d % 4
    x = 2 * high + low
    rings = [((z + n) % 8) * 4 for n in range(8)]
    cores = [core, 1 - core]
    lows = [((x + n) % 4 % 2) * 2 for n in range(4)]
    highs = [((x + n) % 4 // 2) * 4 for n in range(4)]
    columns_y = [(y + n) % 4 for n in range(4)]

    def everyone(act):
        for dz, dy, dx, dc in far_first():
            act(rings[dz] + lows[dx] + cores[dc], highs[dx] + columns_y[dy])

    barrier = pltpu.get_barrier_semaphore()
    everyone(lambda w_to, d_to: pl.semaphore_signal(barrier, 1, device_id=(w_to, d_to), device_id_type=MESH))
    pairs = (
        (slip_hbm, slip_ref),
        (mask_hbm, mask_ref),
        (real_hbm, real_ref),
        (slice_hbm, slice_ref),
        (layer_hbm, layer_ref),
        (material_hbm, material_ref),
        (twiddle_hbm, twiddle_ref),
        (complex_hbm, complex_ref),
    )
    copies = [pltpu.make_async_copy(a, b, input_sem.at[n]) for n, (a, b) in enumerate(pairs)]
    for copy in copies:
        copy.start()
    for copy in copies[:3]:
        copy.wait()
    forward_rows(mask_ref, slip_ref, real_ref, rows_ref)
    sent_ref[...] = rows_ref[...].reshape(sent_ref.shape).astype(jnp.int32).astype(jnp.int16)
    pl.semaphore_wait(barrier, DEVICES - 1)

    def exchange(source, target, number):
        def send(w_to, d_to):
            pltpu.make_async_remote_copy(
                source.at[w_to * 8 + d_to],
                target.at[me],
                send_sem.at[number],
                take_sem.at[number],
                device_id=(w_to, d_to),
                device_id_type=MESH,
            ).start()

        everyone(send)
        own = pltpu.make_async_copy(source.at[me], target.at[me], copy_sem.at[number])
        own.start()
        return own

    def finish(own, source, target, number):
        own.wait()
        most = pl.ds(0, DEVICES - 1)
        pltpu.make_async_copy(source.at[most], target.at[most], send_sem.at[number]).wait()
        pltpu.make_async_copy(source.at[most], target.at[most], take_sem.at[number]).wait()

    own = exchange(sent_ref, got_ref, 0)
    for copy in copies[3:]:
        copy.wait()
    columns = depths(slice_ref, layer_ref, material_ref)
    prepare(me, columns, wave_ref, grow_ref, fall_ref)
    finish(own, sent_ref, got_ref, 0)
    rows_ref[...] = got_ref[...].astype(jnp.int32).astype(F32).reshape(rows_ref.shape)
    middle(
        me,
        columns,
        complex_ref,
        twiddle_ref,
        rows_ref,
        rows_ref,
        left_ref,
        spec_ref,
        edge_ref,
        suffix_ref,
        trac_ref,
        wave_ref,
        grow_ref,
        fall_ref,
    )
    send_ref[...] = rows_ref[...].reshape(send_ref.shape).astype(BF16)
    own = exchange(send_ref, take_ref, 1)
    finish(own, send_ref, take_ref, 1)
    rows_ref[...] = take_ref[...].astype(F32).reshape(rows_ref.shape)
    inverse_rows(real_ref, rows_ref, out_ref)


def spec(space=VMEM):
    return pl.BlockSpec(memory_space=space)


def shards(slip_field, slip_mask, slice_layer, layer_material, materials):
    real_dft, complex_dft, twiddle = tables()
    pin = functools.partial(pltpu.with_memory_space_constraint, memory_space=pltpu.HBM)
    result = pl.pallas_call(
        fused,
        out_shape=jax.ShapeDtypeStruct((32, GRID), F32),
        in_specs=[spec(pltpu.HBM)] * 8,
        out_specs=spec(),
        scratch_shapes=[
            VMEM((2, 32), jnp.int32),
            VMEM((128, GRID), BF16),
            SMEM((NZ,), jnp.int32),
            SMEM((16,), jnp.int32),
            SMEM((3, 8), F32),
            VMEM((16, 128), F32),
            VMEM((2, GRID, HALF), BF16),
            VMEM((2, QUARTER, QUARTER), BF16),
            VMEM((4 * DEVICES, 128), F32),
            VMEM((DEVICES, 4, 128), jnp.int16),
            VMEM((DEVICES, 4, 128), jnp.int16),
            VMEM((DEVICES, 4, 128), BF16),
            VMEM((DEVICES, 4, 128), BF16),
            VMEM((2, 768, 128), F32),
            VMEM((768, 256), F32),
            VMEM((R, 6, 8, 128), F32),
            VMEM((R, 8, 8, 128), F32),
            VMEM((2, 384, 128), F32),
            VMEM((3, 6, 8, 128), F32),
            VMEM((3, S + R, 8, 128), F32),
            VMEM((3, S + R, 8, 128), F32),
            pltpu.SemaphoreType.DMA((8,)),
            pltpu.SemaphoreType.DMA((2,)),
            pltpu.SemaphoreType.DMA((2,)),
            pltpu.SemaphoreType.DMA((2,)),
        ],
        compiler_params=pltpu.CompilerParams(collective_id=0, has_side_effects=True, vmem_limit_bytes=50000000),
        name="fused",
    )(
        *map(
            pin,
            (
                slip_mask.reshape((2, 32)),
                slip_field.reshape((128, GRID)),
                slice_layer,
                layer_material,
                materials,
                jnp.asarray(twiddle),
                jnp.asarray(real_dft),
                jnp.asarray(complex_dft),
            ),
        )
    )
    return result.reshape((1, 32, GRID))


def solution(mesh):
    placed = (P("depth", None, "wave", None), P("depth", "wave", None), P(), P(), P())
    return jax.shard_map(
        shards, mesh=mesh, in_specs=placed, out_specs=P("depth", "wave", None), check_vma=False
    )
```

```python
import functools
import math

import jax
import jax.numpy as jnp
import ml_dtypes
import numpy as np
from jax import lax
from jax.experimental import pallas as pl
from jax.experimental.pallas import tpu as pltpu
from jax.sharding import PartitionSpec as P

GRID = 1024
HALF = 512
QUARTER = 256
S = 16
R = 8
NZ = 64
DEVICES = 256
LARGEST = 6.0 * GRID / 32.0
CODE_SCALE = 32700.0 / LARGEST**0.25
WIDEST = 2.0**20
WIDE_SCALE = 32700.0 / WIDEST**0.125
BF16 = jnp.bfloat16
F32 = jnp.float32
VMEM = pltpu.VMEM
SMEM = pltpu.SMEM


def split_table(table):
    high = table.astype(ml_dtypes.bfloat16)
    low = (table - high.astype(np.float64)).astype(ml_dtypes.bfloat16)
    return np.stack([high, low])


def tables():
    j = np.arange(QUARTER, dtype=np.int64)[:, None]
    cell = np.arange(HALF, dtype=np.int64)[None, :]
    rows = []
    for parity in range(2):
        angle = 2.0 * np.pi * (((2 * j + parity) * cell) % GRID) / GRID
        real, imag = np.cos(angle), -np.sin(angle)
        if parity == 0:
            imag[0] = 1.0 - 2.0 * (cell[0] % 2)
        rows += [real, imag]
    real_dft = np.concatenate(rows) / 32.0
    k = np.arange(128, dtype=np.int64)
    angle = 2.0 * np.pi * ((k[:, None] * k[None, :]) % 128) / 128
    cosine, sine = np.cos(angle) / 32.0, np.sin(angle) / 32.0
    complex_dft = np.block([[cosine, -sine], [sine, cosine]])
    turn = 2.0 * np.pi * np.arange(8)[:, None] * k[None, :] / GRID
    twiddle = np.concatenate([np.cos(turn), -np.sin(turn)]).astype(np.float32)
    return split_table(real_dft), split_table(complex_dft), twiddle


def halves(value):
    high = value.astype(BF16)
    return high, (value - high.astype(F32)).astype(BF16)


def dot(left, right, transposed=False):
    dims = (((1,), (1 if transposed else 0,)), ((), ()))
    return lax.dot_general(left, right, dims, preferred_element_type=F32)


def forward_rows(mask_ref, slip_ref, table_ref, out_ref):
    tile = lax.broadcasted_iota(jnp.int32, (32, GRID), 0)
    cell = lax.broadcasted_iota(jnp.int32, (32, GRID), 1)
    spread = (cell // 32 == tile).astype(BF16)
    mask = dot(mask_ref[...].astype(F32).astype(BF16), spread)
    slip = slip_ref[...].astype(F32)
    rows = slip.shape[0] // 2
    cells = jnp.concatenate([slip[:rows] * mask[0:1], slip[rows:] * mask[1:2]], axis=0)
    near, far = cells[:, :HALF], cells[:, HALF:]
    for parity, combined in enumerate((near + far, near - far)):
        high, low = halves(combined)
        part = slice(parity * HALF, (parity + 1) * HALF)
        result = (
            dot(table_ref[0, part], high, True)
            + dot(table_ref[0, part], low, True)
            + dot(table_ref[1, part], high, True)
        )
        for imag in range(2):
            out_ref[pl.ds(2 * parity + imag, QUARTER, stride=4), :] = encode(
                result[imag * QUARTER : (imag + 1) * QUARTER]
            )


def swap_groups(items):
    lane = lax.broadcasted_iota(jnp.int32, items[0].shape, 1)
    for width in (2, 1):
        size = 32 * width
        upper = (lane // size) % 2 == 1
        out = list(items)
        for a in range(4):
            if a & width:
                continue
            b = a | width
            first, second = items[a], items[b]
            out[a] = jnp.where(upper, pltpu.roll(second, size, 1), first)
            out[b] = jnp.where(upper, second, pltpu.roll(first, 128 - size, 1))
        items = out
    return items


def encode(value):
    code = jnp.sqrt(jnp.sqrt(jnp.abs(value))) * CODE_SCALE + 0.5
    return jnp.where(value < 0.0, -code, code)


def encode_wide(value):
    size = jnp.maximum(jnp.abs(value), 1e-30)
    code = jnp.exp2(jnp.log2(size) * 0.125 + math.log2(WIDE_SCALE)) + 0.5
    return jnp.where(value < 0.0, -code, code)


def decode_wide(code):
    square = code * jnp.abs(code)
    fourth = square * jnp.abs(square)
    return fourth * jnp.abs(fourth) * (1.0 / WIDE_SCALE) ** 8


def decode(code):
    return (code * jnp.abs(code)) * (code * code) * (1.0 / CODE_SCALE) ** 4


def radix_four(items):
    (r0, i0), (r1, i1), (r2, i2), (r3, i3) = items
    ar, ai, br, bi = r0 + r2, i0 + i2, r0 - r2, i0 - i2
    cr, ci, dr, di = r1 + r3, i1 + i3, r1 - r3, i1 - i3
    return [
        (ar + cr, ai + ci),
        (br + di, bi - dr),
        (ar - cr, ai - ci),
        (br - di, bi + dr),
    ]


def radix_eight(items):
    even, odd = radix_four(items[0::2]), radix_four(items[1::2])
    root = math.sqrt(0.5)
    (r0, i0), (r1, i1), (r2, i2), (r3, i3) = odd
    turned = [(r0, i0), (root * (r1 + i1), root * (i1 - r1)), (i2, -r2), (root * (i3 - r3), -root * (r3 + i3))]
    return [(a[0] + b[0], a[1] + b[1]) for a, b in zip(even, turned)] + [
        (a[0] - b[0], a[1] - b[1]) for a, b in zip(even, turned)
    ]


def times(item, cosine, sine):
    real, imag = item
    return real * cosine - imag * sine, real * sine + imag * cosine


def depths(slice_ref, layer_ref, material_ref):
    center, rigidity, friction = [], [], []
    top = None
    for place in range(NZ):
        kind = layer_ref[slice_ref[place]]
        thickness = jnp.float32(0.1) * material_ref[0, kind]
        top = thickness if top is None else top + thickness
        center.append(top - 0.5 * thickness)
        if place % 8 == 3:
            rigidity.append(material_ref[1, kind])
            friction.append(material_ref[2, kind])
    source = [center[4 * s + 1] for s in range(S)]
    receiver = [center[8 * r + 3] for r in range(R)]
    return source, receiver, rigidity, friction


def wave_arrays(kind, j):
    kx = 8 * lax.broadcasted_iota(jnp.int32, (8, 128), 1) + lax.broadcasted_iota(jnp.int32, (8, 128), 0)
    signed = jnp.where(kx >= HALF, kx - GRID, kx)
    ky = jnp.full((8, 128), -HALF, jnp.int32) if kind == 2 else jnp.full((8, 128), 2 * j + kind, jnp.int32)
    x_wave, y_wave = signed.astype(F32), ky.astype(F32)
    magnitude = jnp.sqrt(x_wave * x_wave + y_wave * y_wave)
    bounded = jnp.maximum(magnitude, 1.0)
    along_x, along_y = x_wave / bounded, y_wave / bounded
    x_edge = signed == -HALF
    y_edge = ky == -HALF
    cross = jnp.where(x_edge != y_edge, 0.0, along_x * along_y)
    odd_x = jnp.where(x_edge, 0.0, along_x)
    odd_y = jnp.where(y_edge, 0.0, along_y)
    wave = 2.0 * math.pi / GRID * magnitude
    return wave, along_x * along_x, cross, along_y * along_y, odd_x, odd_y


def prepare(j, columns, wave_ref, grow_ref, fall_ref, pair_ref):
    source, receiver, rigidity, _ = columns
    double = jnp.where(j == 0, 1.0, 2.0).astype(F32)
    weights = [double, jnp.float32(2.0), 2.0 - double]
    for kind in range(3):
        arrays = wave_arrays(kind, j)
        for n, value in enumerate(arrays):
            wave_ref[kind, n] = value
        for n, z in enumerate(source):
            exponent = arrays[0] * z
            grow_ref[kind, n] = jnp.exp(exponent)
            fall_ref[kind, n] = jnp.exp(-exponent)
        for r in range(R):
            exponent = arrays[0] * receiver[r]
            for n, sign in enumerate((-1.0, 1.0)):
                weighted = (weights[kind] * rigidity[r]) * jnp.exp(sign * exponent)
                pair_ref[kind, r, n] = weighted
                pair_ref[kind, r, 2 + n] = arrays[0] * weighted


def middle(
    j,
    columns,
    table_ref,
    twiddle_ref,
    got_ref,
    out_ref,
    left_ref,
    spec_ref,
    edge_ref,
    suffix_ref,
    trac_ref,
    wave_ref,
    grow_ref,
    fall_ref,
    pair_ref,
):
    source, receiver, rigidity, friction = columns
    keep_imag = jnp.where(j == 0, 0.0, 1.0).astype(F32)
    cosines = [twiddle_ref[a : a + 1, :] for a in range(8)]
    sines = [twiddle_ref[8 + a : 9 + a, :] for a in range(8)]

    loaded = [decode(got_ref[pl.ds(c, DEVICES, stride=4), :]) for c in range(4)]
    blocks = [[[None] * 8 for _ in range(4)] for _ in range(4)]
    for c in range(4):
        for outer in range(8):
            group = swap_groups([loaded[c][(4 * outer + inner) * 8 : (4 * outer + inner) * 8 + 8] for inner in range(4)])
            for g in range(4):
                blocks[c][g][outer] = group[g]
    for g in range(4):
        kinds = [
            [(blocks[0][g][o], blocks[1][g][o] * keep_imag) for o in range(8)],
            [(blocks[2][g][o], blocks[3][g][o]) for o in range(8)],
            [(blocks[1][g][o], jnp.zeros_like(blocks[1][g][o])) for o in range(8)],
        ]
        for kind in range(3):
            mixed = radix_eight(kinds[kind])
            for k0 in range(8):
                real, imag = times(mixed[k0], cosines[k0], sines[k0]) if k0 else mixed[k0]
                place = pl.ds(64 * (4 * kind + g) + k0, 8, stride=8)
                left_ref.at[0][place, :] = real
                left_ref.at[1][place, :] = imag
    high, low = halves(jnp.concatenate([left_ref[0], left_ref[1]], axis=1))
    spectra = dot(high, table_ref[0]) + dot(low, table_ref[0]) + dot(high, table_ref[1])
    spec_ref[...] = spectra.astype(BF16).astype(F32)

    def unit(kind, write):
        uu, uv, vv, odd_x, odd_y = [wave_ref[kind, n] for n in range(1, 6)]

        def fields(s):
            rows = [8 * (8 * (4 * kind + 2 * (s % 2) + q) + s // 2) for q in range(2)]
            return [spec_ref[row : row + 8, 128 * n : 128 * n + 128] for row in rows for n in range(2)]

        zero = jnp.zeros((8, 128), F32)
        suffix, moment = [zero] * 4, [zero] * 4
        for s in reversed(range(S)):
            decay = fall_ref[kind, s]
            scaled = [decay * value for value in fields(s)]
            suffix = [a + b for a, b in zip(suffix, scaled)]
            moment = [a + source[s] * b for a, b in zip(moment, scaled)]
            if s % 2 == 1:
                for n in range(4):
                    suffix_ref[s // 2, n] = suffix[n]
                    suffix_ref[s // 2, 4 + n] = moment[n]
        twice = [a + a for a in suffix]
        prefix = suffix
        for s in range(S - 1):
            growth = grow_ref[kind, s]
            scaled = [growth * value for value in fields(s)]
            prefix = [a + b for a, b in zip(prefix, scaled)]
            moment = [a + source[s] * b for a, b in zip(moment, scaled)]
            if s % 2 == 0:
                r = s // 2
                z = receiver[r]
                fall, rise, wave_fall, wave_rise = [pair_ref[kind, r, n] for n in range(4)]
                summed, slope = [], []
                for n in range(4):
                    after, after_moment = suffix_ref[r, n], suffix_ref[r, 4 + n]
                    summed.append(fall * prefix[n] + rise * after)
                    slope.append(
                        wave_fall * (z * (prefix[n] - twice[n]) - moment[n]) + wave_rise * (after_moment - z * after)
                    )
                along = [a - b for a, b in zip(summed, slope)]
                write(
                    r,
                    [
                        summed[0] - uu * slope[0] - uv * slope[2],
                        summed[1] - uu * slope[1] - uv * slope[3],
                        summed[2] - uv * slope[0] - vv * slope[2],
                        summed[3] - uv * slope[1] - vv * slope[3],
                        -friction[r] * (odd_x * along[1] + odd_y * along[3]),
                        friction[r] * (odd_x * along[0] + odd_y * along[2]),
                    ],
                )

    def write_edge(r, values):
        for n in range(6):
            edge_ref[r, n] = values[n]

    unit(2, write_edge)
    for p in range(2):

        def write_main(r, values):
            for c in range(3):
                real, imag = values[2 * c], values[2 * c + 1]
                if p == 0:
                    real, imag = real - edge_ref[r, 2 * c + 1], imag + edge_ref[r, 2 * c]
                place = pl.ds(64 * (2 * c + p) + r, 8, stride=8)
                trac_ref.at[0][place, :] = real
                trac_ref.at[1][place, :] = -imag

        unit(p, write_main)

    high, low = halves(jnp.concatenate([trac_ref[0], trac_ref[1]], axis=1))
    turned = dot(high, table_ref[0]) + dot(low, table_ref[0]) + dot(high, table_ref[1])
    for c in range(3):
        fields = []
        for p in range(2):
            items = []
            for k0 in range(8):
                row = 64 * (2 * c + p) + 8 * k0
                item = (turned[row : row + 8, :128], turned[row : row + 8, 128:])
                items.append(times(item, cosines[k0], sines[k0]) if k0 else item)
            mixed = radix_eight(items)
            fields.append([item[0] for item in mixed])
            fields.append([-item[1] for item in mixed])
        for outer in range(8):
            group = swap_groups([fields[n][outer] for n in range(4)])
            for inner in range(4):
                w = 4 * outer + inner
                out_ref[pl.ds(32 * w + c, 8, stride=4), :] = encode_wide(group[inner])


def inverse_rows(table_ref, got_ref, out_ref):
    flipped = [decode_wide(got_ref[pl.ds(c, DEVICES, stride=4), :]).T for c in range(3)]
    parts = []
    for parity in range(2):
        rows = []
        for c in range(3):
            real = flipped[c][64 * parity : 64 * parity + 32]
            imag = flipped[c][64 * parity + 32 : 64 * parity + 64]
            rows.append(jnp.concatenate([real, imag], axis=1))
        high, low = halves(jnp.concatenate(rows, axis=0))
        part = slice(parity * HALF, (parity + 1) * HALF)
        parts.append(
            dot(high, table_ref[0, part]) + dot(low, table_ref[0, part]) + dot(high, table_ref[1, part])
        )
    for side, stress in enumerate((parts[0] + parts[1], parts[0] - parts[1])):
        first, second, third = stress[0:32], stress[32:64], stress[64:96]
        out_ref[:, side * HALF : (side + 1) * HALF] = jnp.sqrt(first * first + second * second + 1.0) + third


MESH = pl.DeviceIdType.MESH


def far_first():
    places = [(z, y, x, c) for z in range(8) for y in range(4) for x in range(4) for c in range(2)][1:]

    def rank(place):
        z, y, x, c = place
        hops = min(z, 8 - z) + min(y, 4 - y) + min(x, 4 - x)
        return -hops, (z * 89 + y * 37 + x * 53 + c * 101) % 61, place

    return sorted(places, key=rank)


def fused(
    mask_hbm,
    slip_hbm,
    slice_hbm,
    layer_hbm,
    material_hbm,
    twiddle_hbm,
    real_hbm,
    complex_hbm,
    out_ref,
    mask_ref,
    slip_ref,
    slice_ref,
    layer_ref,
    material_ref,
    twiddle_ref,
    real_ref,
    complex_ref,
    rows_ref,
    sent_ref,
    got_ref,
    send_ref,
    take_ref,
    left_ref,
    spec_ref,
    edge_ref,
    suffix_ref,
    trac_ref,
    wave_ref,
    grow_ref,
    fall_ref,
    pair_ref,
    input_sem,
    copy_sem,
    send_sem,
    take_sem,
):
    w, d = lax.axis_index("wave"), lax.axis_index("depth")
    me = w * 8 + d
    z, low, core = w // 4, (w // 2) % 2, w % 2
    high, y = d // 4, d % 4
    x = 2 * high + low
    rings = [((z + n) % 8) * 4 for n in range(8)]
    cores = [core, 1 - core]
    lows = [((x + n) % 4 % 2) * 2 for n in range(4)]
    highs = [((x + n) % 4 // 2) * 4 for n in range(4)]
    columns_y = [(y + n) % 4 for n in range(4)]

    def everyone(act, part=slice(None)):
        for dz, dy, dx, dc in far_first()[part]:
            act(rings[dz] + lows[dx] + cores[dc], highs[dx] + columns_y[dy])

    barrier = pltpu.get_barrier_semaphore()

    def greet(w_to, d_to):
        pl.semaphore_signal(barrier, 1, device_id=(w_to, d_to), device_id_type=MESH)

    everyone(greet, slice(0, 64))
    pairs = (
        (slip_hbm, slip_ref),
        (mask_hbm, mask_ref),
        (real_hbm, real_ref),
        (slice_hbm, slice_ref),
        (layer_hbm, layer_ref),
        (material_hbm, material_ref),
        (twiddle_hbm, twiddle_ref),
        (complex_hbm, complex_ref),
    )
    copies = [pltpu.make_async_copy(a, b, input_sem.at[n]) for n, (a, b) in enumerate(pairs)]
    for copy in copies:
        copy.start()
    everyone(greet, slice(64, None))
    for copy in copies[:3]:
        copy.wait()
    forward_rows(mask_ref, slip_ref, real_ref, rows_ref)
    sent_ref[...] = rows_ref[...].reshape(sent_ref.shape).astype(jnp.int32).astype(jnp.int16)
    pl.semaphore_wait(barrier, DEVICES - 1)

    def exchange(source, target, number):
        def send(w_to, d_to):
            pltpu.make_async_remote_copy(
                source.at[w_to * 8 + d_to],
                target.at[me],
                send_sem.at[number],
                take_sem.at[number],
                device_id=(w_to, d_to),
                device_id_type=MESH,
            ).start()

        everyone(send)
        own = pltpu.make_async_copy(source.at[me], target.at[me], copy_sem.at[number])
        own.start()
        return own

    most = pl.ds(0, DEVICES - 1)

    def arrived(own, source, target, number):
        own.wait()
        pltpu.make_async_copy(source.at[most], target.at[most], take_sem.at[number]).wait()

    def left(source, target, number):
        pltpu.make_async_copy(source.at[most], target.at[most], send_sem.at[number]).wait()

    own = exchange(sent_ref, got_ref, 0)
    for copy in copies[3:]:
        copy.wait()
    columns = depths(slice_ref, layer_ref, material_ref)
    prepare(me, columns, wave_ref, grow_ref, fall_ref, pair_ref)
    arrived(own, sent_ref, got_ref, 0)
    rows_ref[...] = got_ref[...].astype(jnp.int32).astype(F32).reshape(rows_ref.shape)
    middle(
        me,
        columns,
        complex_ref,
        twiddle_ref,
        rows_ref,
        rows_ref,
        left_ref,
        spec_ref,
        edge_ref,
        suffix_ref,
        trac_ref,
        wave_ref,
        grow_ref,
        fall_ref,
        pair_ref,
    )
    send_ref[...] = rows_ref[...].reshape(send_ref.shape).astype(jnp.int32).astype(jnp.int16)
    own = exchange(send_ref, take_ref, 1)
    arrived(own, send_ref, take_ref, 1)
    rows_ref[...] = take_ref[...].astype(jnp.int32).astype(F32).reshape(rows_ref.shape)
    inverse_rows(real_ref, rows_ref, out_ref)
    left(sent_ref, got_ref, 0)
    left(send_ref, take_ref, 1)


def spec(space=VMEM):
    return pl.BlockSpec(memory_space=space)


def shards(slip_field, slip_mask, slice_layer, layer_material, materials):
    real_dft, complex_dft, twiddle = tables()
    pin = functools.partial(pltpu.with_memory_space_constraint, memory_space=pltpu.HBM)
    result = pl.pallas_call(
        fused,
        out_shape=jax.ShapeDtypeStruct((32, GRID), F32),
        in_specs=[spec(pltpu.HBM)] * 8,
        out_specs=spec(),
        scratch_shapes=[
            VMEM((2, 32), jnp.int32),
            VMEM((128, GRID), BF16),
            SMEM((NZ,), jnp.int32),
            SMEM((16,), jnp.int32),
            SMEM((3, 8), F32),
            VMEM((16, 128), F32),
            VMEM((2, GRID, HALF), BF16),
            VMEM((2, QUARTER, QUARTER), BF16),
            VMEM((4 * DEVICES, 128), F32),
            VMEM((DEVICES, 4, 128), jnp.int16),
            VMEM((DEVICES, 4, 128), jnp.int16),
            VMEM((DEVICES, 4, 128), jnp.int16),
            VMEM((DEVICES, 4, 128), jnp.int16),
            VMEM((2, 768, 128), F32),
            VMEM((768, 256), F32),
            VMEM((R, 6, 8, 128), F32),
            VMEM((R, 8, 8, 128), F32),
            VMEM((2, 384, 128), F32),
            VMEM((3, 6, 8, 128), F32),
            VMEM((3, S, 8, 128), F32),
            VMEM((3, S, 8, 128), F32),
            VMEM((3, R, 4, 8, 128), F32),
            pltpu.SemaphoreType.DMA((8,)),
            pltpu.SemaphoreType.DMA((2,)),
            pltpu.SemaphoreType.DMA((2,)),
            pltpu.SemaphoreType.DMA((2,)),
        ],
        compiler_params=pltpu.CompilerParams(collective_id=0, has_side_effects=True, vmem_limit_bytes=50000000),
        name="fused",
    )(
        *map(
            pin,
            (
                slip_mask.reshape((2, 32)),
                slip_field.reshape((128, GRID)),
                slice_layer,
                layer_material,
                materials,
                jnp.asarray(twiddle),
                jnp.asarray(real_dft),
                jnp.asarray(complex_dft),
            ),
        )
    )
    return result.reshape((1, 32, GRID))


def solution(mesh):
    placed = (P("depth", None, "wave", None), P("depth", "wave", None), P(), P(), P())
    return jax.shard_map(
        shards, mesh=mesh, in_specs=placed, out_specs=P("depth", "wave", None), check_vma=False
    )
```

```python
import functools
import math

import jax
import jax.numpy as jnp
import ml_dtypes
import numpy as np
from jax import lax
from jax.experimental import pallas as pl
from jax.experimental.pallas import tpu as pltpu
from jax.sharding import PartitionSpec as P

GRID = 1024
HALF = 512
QUARTER = 256
S = 16
R = 8
NZ = 64
DEVICES = 256
LARGEST = 6.0 * GRID / 32.0
CODE_SCALE = 32700.0 / LARGEST**0.25
WIDEST = 2.0**20
WIDE_SCALE = 32700.0 / WIDEST**0.125
BF16 = jnp.bfloat16
F32 = jnp.float32
VMEM = pltpu.VMEM
SMEM = pltpu.SMEM


def split_table(table):
    high = table.astype(ml_dtypes.bfloat16)
    low = (table - high.astype(np.float64)).astype(ml_dtypes.bfloat16)
    return np.stack([high, low])


def tables():
    j = np.arange(QUARTER, dtype=np.int64)[:, None]
    cell = np.arange(HALF, dtype=np.int64)[None, :]
    rows = []
    for parity in range(2):
        angle = 2.0 * np.pi * (((2 * j + parity) * cell) % GRID) / GRID
        real, imag = np.cos(angle), -np.sin(angle)
        if parity == 0:
            imag[0] = 1.0 - 2.0 * (cell[0] % 2)
        rows += [real, imag]
    real_dft = np.concatenate(rows) / 32.0
    k = np.arange(128, dtype=np.int64)
    angle = 2.0 * np.pi * ((k[:, None] * k[None, :]) % 128) / 128
    cosine, sine = np.cos(angle) / 32.0, np.sin(angle) / 32.0
    complex_dft = np.block([[cosine, -sine], [sine, cosine]])
    turn = 2.0 * np.pi * np.arange(8)[:, None] * k[None, :] / GRID
    twiddle = np.concatenate([np.cos(turn), -np.sin(turn)]).astype(np.float32)
    return split_table(real_dft), split_table(complex_dft), twiddle


def halves(value):
    high = value.astype(BF16)
    return high, (value - high.astype(F32)).astype(BF16)


def dot(left, right, transposed=False):
    dims = (((1,), (1 if transposed else 0,)), ((), ()))
    return lax.dot_general(left, right, dims, preferred_element_type=F32)


def forward_rows(mask_ref, slip_ref, table_ref, out_ref):
    tile = lax.broadcasted_iota(jnp.int32, (32, GRID), 0)
    cell = lax.broadcasted_iota(jnp.int32, (32, GRID), 1)
    spread = (cell // 32 == tile).astype(BF16)
    mask = dot(mask_ref[...].astype(F32).astype(BF16), spread)
    slip = slip_ref[...].astype(F32)
    rows = slip.shape[0] // 2
    cells = jnp.concatenate([slip[:rows] * mask[0:1], slip[rows:] * mask[1:2]], axis=0)
    near, far = cells[:, :HALF], cells[:, HALF:]
    for parity, combined in enumerate((near + far, near - far)):
        high, low = halves(combined)
        part = slice(parity * HALF, (parity + 1) * HALF)
        result = (
            dot(table_ref[0, part], high, True)
            + dot(table_ref[0, part], low, True)
            + dot(table_ref[1, part], high, True)
        )
        for imag in range(2):
            out_ref[pl.ds(2 * parity + imag, QUARTER, stride=4), :] = encode(
                result[imag * QUARTER : (imag + 1) * QUARTER]
            )


def swap_groups(items):
    lane = lax.broadcasted_iota(jnp.int32, items[0].shape, 1)
    for width in (2, 1):
        size = 32 * width
        upper = (lane // size) % 2 == 1
        out = list(items)
        for a in range(4):
            if a & width:
                continue
            b = a | width
            first, second = items[a], items[b]
            out[a] = jnp.where(upper, pltpu.roll(second, size, 1), first)
            out[b] = jnp.where(upper, second, pltpu.roll(first, 128 - size, 1))
        items = out
    return items


def encode(value):
    code = jnp.sqrt(jnp.sqrt(jnp.abs(value))) * CODE_SCALE + 0.5
    return jnp.where(value < 0.0, -code, code)


def encode_wide(value):
    size = jnp.maximum(jnp.abs(value), 1e-30)
    code = jnp.exp2(jnp.log2(size) * 0.125 + math.log2(WIDE_SCALE)) + 0.5
    return jnp.where(value < 0.0, -code, code)


def decode_wide(code):
    square = code * jnp.abs(code)
    fourth = square * jnp.abs(square)
    return fourth * jnp.abs(fourth) * (1.0 / WIDE_SCALE) ** 8


def decode(code):
    return (code * jnp.abs(code)) * (code * code) * (1.0 / CODE_SCALE) ** 4


def radix_four(items):
    (r0, i0), (r1, i1), (r2, i2), (r3, i3) = items
    ar, ai, br, bi = r0 + r2, i0 + i2, r0 - r2, i0 - i2
    cr, ci, dr, di = r1 + r3, i1 + i3, r1 - r3, i1 - i3
    return [
        (ar + cr, ai + ci),
        (br + di, bi - dr),
        (ar - cr, ai - ci),
        (br - di, bi + dr),
    ]


def radix_eight(items):
    even, odd = radix_four(items[0::2]), radix_four(items[1::2])
    root = math.sqrt(0.5)
    (r0, i0), (r1, i1), (r2, i2), (r3, i3) = odd
    turned = [(r0, i0), (root * (r1 + i1), root * (i1 - r1)), (i2, -r2), (root * (i3 - r3), -root * (r3 + i3))]
    return [(a[0] + b[0], a[1] + b[1]) for a, b in zip(even, turned)] + [
        (a[0] - b[0], a[1] - b[1]) for a, b in zip(even, turned)
    ]


def times(item, cosine, sine):
    real, imag = item
    return real * cosine - imag * sine, real * sine + imag * cosine


def depths(slice_ref, layer_ref, material_ref):
    center, rigidity, friction = [], [], []
    top = None
    for place in range(NZ):
        kind = layer_ref[slice_ref[place]]
        thickness = jnp.float32(0.1) * material_ref[0, kind]
        top = thickness if top is None else top + thickness
        center.append(top - 0.5 * thickness)
        if place % 8 == 3:
            rigidity.append(material_ref[1, kind])
            friction.append(material_ref[2, kind])
    source = [center[4 * s + 1] for s in range(S)]
    receiver = [center[8 * r + 3] for r in range(R)]
    return source, receiver, rigidity, friction


def wave_arrays(kind, j):
    kx = 8 * lax.broadcasted_iota(jnp.int32, (8, 128), 1) + lax.broadcasted_iota(jnp.int32, (8, 128), 0)
    signed = jnp.where(kx >= HALF, kx - GRID, kx)
    ky = jnp.full((8, 128), -HALF, jnp.int32) if kind == 2 else jnp.full((8, 128), 2 * j + kind, jnp.int32)
    x_wave, y_wave = signed.astype(F32), ky.astype(F32)
    magnitude = jnp.sqrt(x_wave * x_wave + y_wave * y_wave)
    bounded = jnp.maximum(magnitude, 1.0)
    along_x, along_y = x_wave / bounded, y_wave / bounded
    x_edge = signed == -HALF
    y_edge = ky == -HALF
    cross = jnp.where(x_edge != y_edge, 0.0, along_x * along_y)
    odd_x = jnp.where(x_edge, 0.0, along_x)
    odd_y = jnp.where(y_edge, 0.0, along_y)
    wave = 2.0 * math.pi / GRID * magnitude
    return wave, along_x * along_x, cross, along_y * along_y, odd_x, odd_y


def prepare(j, columns, wave_ref, grow_ref, fall_ref, pair_ref):
    source, receiver, rigidity, _ = columns
    double = jnp.where(j == 0, 1.0, 2.0).astype(F32)
    weights = [double, jnp.float32(2.0), 2.0 - double]
    for kind in range(3):
        arrays = wave_arrays(kind, j)
        for n, value in enumerate(arrays):
            wave_ref[kind, n] = value
        for n, z in enumerate(source):
            exponent = arrays[0] * z
            grow_ref[kind, n] = jnp.exp(exponent)
            fall_ref[kind, n] = jnp.exp(-exponent)
        for r in range(R):
            exponent = arrays[0] * receiver[r]
            for n, sign in enumerate((-1.0, 1.0)):
                weighted = (weights[kind] * rigidity[r]) * jnp.exp(sign * exponent)
                pair_ref[kind, r, n] = weighted
                pair_ref[kind, r, 2 + n] = arrays[0] * weighted


def middle(
    j,
    columns,
    table_ref,
    twiddle_ref,
    got_ref,
    out_ref,
    left_ref,
    spec_ref,
    edge_ref,
    suffix_ref,
    trac_ref,
    wave_ref,
    grow_ref,
    fall_ref,
    pair_ref,
):
    source, receiver, rigidity, friction = columns
    keep_imag = jnp.where(j == 0, 0.0, 1.0).astype(F32)
    cosines = [twiddle_ref[a : a + 1, :] for a in range(8)]
    sines = [twiddle_ref[8 + a : 9 + a, :] for a in range(8)]

    loaded = [decode(got_ref[pl.ds(c, DEVICES, stride=4), :]) for c in range(4)]
    blocks = [[[None] * 8 for _ in range(4)] for _ in range(4)]
    for c in range(4):
        for outer in range(8):
            group = swap_groups([loaded[c][(4 * outer + inner) * 8 : (4 * outer + inner) * 8 + 8] for inner in range(4)])
            for g in range(4):
                blocks[c][g][outer] = group[g]
    for g in range(4):
        kinds = [
            [(blocks[0][g][o], blocks[1][g][o] * keep_imag) for o in range(8)],
            [(blocks[2][g][o], blocks[3][g][o]) for o in range(8)],
            [(blocks[1][g][o], jnp.zeros_like(blocks[1][g][o])) for o in range(8)],
        ]
        for kind in range(3):
            mixed = radix_eight(kinds[kind])
            for k0 in range(8):
                real, imag = times(mixed[k0], cosines[k0], sines[k0]) if k0 else mixed[k0]
                place = pl.ds(64 * (4 * kind + g) + k0, 8, stride=8)
                left_ref.at[0][place, :] = real
                left_ref.at[1][place, :] = imag
    high, low = halves(jnp.concatenate([left_ref[0], left_ref[1]], axis=1))
    spectra = dot(high, table_ref[0]) + dot(low, table_ref[0]) + dot(high, table_ref[1])
    spec_ref[...] = spectra.astype(BF16).astype(F32)

    def unit(kind, write):
        uu, uv, vv, odd_x, odd_y = [wave_ref[kind, n] for n in range(1, 6)]

        def fields(s):
            rows = [8 * (8 * (4 * kind + 2 * (s % 2) + q) + s // 2) for q in range(2)]
            return [spec_ref[row : row + 8, 128 * n : 128 * n + 128] for row in rows for n in range(2)]

        zero = jnp.zeros((8, 128), F32)
        suffix, moment = [zero] * 4, [zero] * 4
        for s in reversed(range(S)):
            decay = fall_ref[kind, s]
            scaled = [decay * value for value in fields(s)]
            suffix = [a + b for a, b in zip(suffix, scaled)]
            moment = [a + source[s] * b for a, b in zip(moment, scaled)]
            if s % 2 == 1:
                for n in range(4):
                    suffix_ref[s // 2, n] = suffix[n]
                    suffix_ref[s // 2, 4 + n] = moment[n]
        twice = [a + a for a in suffix]
        prefix = suffix
        for s in range(S - 1):
            growth = grow_ref[kind, s]
            scaled = [growth * value for value in fields(s)]
            prefix = [a + b for a, b in zip(prefix, scaled)]
            moment = [a + source[s] * b for a, b in zip(moment, scaled)]
            if s % 2 == 0:
                r = s // 2
                z = receiver[r]
                fall, rise, wave_fall, wave_rise = [pair_ref[kind, r, n] for n in range(4)]
                summed, slope = [], []
                for n in range(4):
                    after, after_moment = suffix_ref[r, n], suffix_ref[r, 4 + n]
                    summed.append(fall * prefix[n] + rise * after)
                    slope.append(
                        wave_fall * (z * (prefix[n] - twice[n]) - moment[n]) + wave_rise * (after_moment - z * after)
                    )
                along = [a - b for a, b in zip(summed, slope)]
                write(
                    r,
                    [
                        summed[0] - uu * slope[0] - uv * slope[2],
                        summed[1] - uu * slope[1] - uv * slope[3],
                        summed[2] - uv * slope[0] - vv * slope[2],
                        summed[3] - uv * slope[1] - vv * slope[3],
                        -friction[r] * (odd_x * along[1] + odd_y * along[3]),
                        friction[r] * (odd_x * along[0] + odd_y * along[2]),
                    ],
                )

    def write_edge(r, values):
        for n in range(6):
            edge_ref[r, n] = values[n]

    unit(2, write_edge)
    for p in range(2):

        def write_main(r, values):
            for c in range(3):
                real, imag = values[2 * c], values[2 * c + 1]
                if p == 0:
                    real, imag = real - edge_ref[r, 2 * c + 1], imag + edge_ref[r, 2 * c]
                place = pl.ds(64 * (2 * c + p) + r, 8, stride=8)
                trac_ref.at[0][place, :] = real
                trac_ref.at[1][place, :] = -imag

        unit(p, write_main)

    high, low = halves(jnp.concatenate([trac_ref[0], trac_ref[1]], axis=1))
    turned = dot(high, table_ref[0]) + dot(low, table_ref[0]) + dot(high, table_ref[1])
    for c in range(3):
        fields = []
        for p in range(2):
            items = []
            for k0 in range(8):
                row = 64 * (2 * c + p) + 8 * k0
                item = (turned[row : row + 8, :128], turned[row : row + 8, 128:])
                items.append(times(item, cosines[k0], sines[k0]) if k0 else item)
            mixed = radix_eight(items)
            fields.append([item[0] for item in mixed])
            fields.append([-item[1] for item in mixed])
        for outer in range(8):
            group = swap_groups([fields[n][outer] for n in range(4)])
            for inner in range(4):
                w = 4 * outer + inner
                out_ref[pl.ds(32 * w + c, 8, stride=4), :] = encode_wide(group[inner])


def inverse_rows(table_ref, got_ref, out_ref):
    flipped = [decode_wide(got_ref[pl.ds(c, DEVICES, stride=4), :]).T for c in range(3)]
    parts = []
    for parity in range(2):
        rows = []
        for c in range(3):
            real = flipped[c][64 * parity : 64 * parity + 32]
            imag = flipped[c][64 * parity + 32 : 64 * parity + 64]
            rows.append(jnp.concatenate([real, imag], axis=1))
        high, low = halves(jnp.concatenate(rows, axis=0))
        part = slice(parity * HALF, (parity + 1) * HALF)
        parts.append(
            dot(high, table_ref[0, part]) + dot(low, table_ref[0, part]) + dot(high, table_ref[1, part])
        )
    for side, stress in enumerate((parts[0] + parts[1], parts[0] - parts[1])):
        first, second, third = stress[0:32], stress[32:64], stress[64:96]
        out_ref[:, side * HALF : (side + 1) * HALF] = jnp.sqrt(first * first + second * second + 1.0) + third


LOGICAL = pl.DeviceIdType.LOGICAL


def far_first():
    places = [(z, y, x, c) for z in range(8) for y in range(4) for x in range(4) for c in range(2)][1:]

    def rank(place):
        z, y, x, c = place
        hops = min(z, 8 - z) + min(y, 4 - y) + min(x, 4 - x)
        return -hops, (z * 89 + y * 37 + x * 53 + c * 101) % 61, place

    return sorted(places, key=rank)


def fused(
    mask_hbm,
    slip_hbm,
    slice_hbm,
    layer_hbm,
    material_hbm,
    twiddle_hbm,
    real_hbm,
    complex_hbm,
    out_ref,
    mask_ref,
    slip_ref,
    slice_ref,
    layer_ref,
    material_ref,
    twiddle_ref,
    real_ref,
    complex_ref,
    rows_ref,
    sent_ref,
    got_ref,
    send_ref,
    take_ref,
    left_ref,
    spec_ref,
    edge_ref,
    suffix_ref,
    trac_ref,
    wave_ref,
    grow_ref,
    fall_ref,
    pair_ref,
    input_sem,
    copy_sem,
    send_sem,
    take_sem,
):
    w, d = lax.axis_index("wave"), lax.axis_index("depth")
    me = w * 8 + d
    z, low, core = w // 4, (w // 2) % 2, w % 2
    high, y = d // 4, d % 4
    x = 2 * high + low
    rings = [((z + n) % 8) * 4 for n in range(8)]
    cores = [core, 1 - core]
    lows = [((x + n) % 4 % 2) * 2 for n in range(4)]
    highs = [((x + n) % 4 // 2) * 4 for n in range(4)]
    columns_y = [(y + n) % 4 for n in range(4)]
    depth_first = [[8 * (ring + c) for c in cores] for ring in rings]
    sheets = [[8 * low_to + high_to + y_to for low_to, high_to in zip(lows, highs)] for y_to in columns_y]

    def everyone(act, part=slice(None)):
        for dz, dy, dx, dc in far_first()[part]:
            act(depth_first[dz][dc] + sheets[dy][dx])

    barrier = pltpu.get_barrier_semaphore()

    def greet(to):
        pl.semaphore_signal(barrier, 1, device_id=to, device_id_type=LOGICAL)

    everyone(greet, slice(0, 64))
    pairs = (
        (slip_hbm, slip_ref),
        (mask_hbm, mask_ref),
        (real_hbm, real_ref),
        (slice_hbm, slice_ref),
        (layer_hbm, layer_ref),
        (material_hbm, material_ref),
        (twiddle_hbm, twiddle_ref),
        (complex_hbm, complex_ref),
    )
    copies = [pltpu.make_async_copy(a, b, input_sem.at[n]) for n, (a, b) in enumerate(pairs)]
    for copy in copies:
        copy.start()
    everyone(greet, slice(64, None))
    for copy in copies[:3]:
        copy.wait()
    forward_rows(mask_ref, slip_ref, real_ref, rows_ref)
    sent_ref[...] = rows_ref[...].reshape(sent_ref.shape).astype(jnp.int32).astype(jnp.int16)
    pl.semaphore_wait(barrier, DEVICES - 1)

    def exchange(source, target, number):
        def send(to):
            pltpu.make_async_remote_copy(
                source.at[to],
                target.at[me],
                send_sem.at[number],
                take_sem.at[number],
                device_id=to,
                device_id_type=LOGICAL,
            ).start()

        everyone(send)
        own = pltpu.make_async_copy(source.at[me], target.at[me], copy_sem.at[number])
        own.start()
        return own

    most = pl.ds(0, DEVICES - 1)

    def arrived(own, source, target, number):
        own.wait()
        pltpu.make_async_copy(source.at[most], target.at[most], take_sem.at[number]).wait()

    def left(source, target, number):
        pltpu.make_async_copy(source.at[most], target.at[most], send_sem.at[number]).wait()

    own = exchange(sent_ref, got_ref, 0)
    for copy in copies[3:]:
        copy.wait()
    columns = depths(slice_ref, layer_ref, material_ref)
    prepare(me, columns, wave_ref, grow_ref, fall_ref, pair_ref)
    arrived(own, sent_ref, got_ref, 0)
    rows_ref[...] = got_ref[...].astype(jnp.int32).astype(F32).reshape(rows_ref.shape)
    middle(
        me,
        columns,
        complex_ref,
        twiddle_ref,
        rows_ref,
        rows_ref,
        left_ref,
        spec_ref,
        edge_ref,
        suffix_ref,
        trac_ref,
        wave_ref,
        grow_ref,
        fall_ref,
        pair_ref,
    )
    send_ref[...] = rows_ref[...].reshape(send_ref.shape).astype(jnp.int32).astype(jnp.int16)
    own = exchange(send_ref, take_ref, 1)
    arrived(own, send_ref, take_ref, 1)
    rows_ref[...] = take_ref[...].astype(jnp.int32).astype(F32).reshape(rows_ref.shape)
    inverse_rows(real_ref, rows_ref, out_ref)
    left(sent_ref, got_ref, 0)
    left(send_ref, take_ref, 1)


def spec(space=VMEM):
    return pl.BlockSpec(memory_space=space)


def shards(slip_field, slip_mask, slice_layer, layer_material, materials):
    real_dft, complex_dft, twiddle = tables()
    pin = functools.partial(pltpu.with_memory_space_constraint, memory_space=pltpu.HBM)
    result = pl.pallas_call(
        fused,
        out_shape=jax.ShapeDtypeStruct((32, GRID), F32),
        in_specs=[spec(pltpu.HBM)] * 8,
        out_specs=spec(),
        scratch_shapes=[
            VMEM((2, 32), jnp.int32),
            VMEM((128, GRID), BF16),
            SMEM((NZ,), jnp.int32),
            SMEM((16,), jnp.int32),
            SMEM((3, 8), F32),
            VMEM((16, 128), F32),
            VMEM((2, GRID, HALF), BF16),
            VMEM((2, QUARTER, QUARTER), BF16),
            VMEM((4 * DEVICES, 128), F32),
            VMEM((DEVICES, 4, 128), jnp.int16),
            VMEM((DEVICES, 4, 128), jnp.int16),
            VMEM((DEVICES, 4, 128), jnp.int16),
            VMEM((DEVICES, 4, 128), jnp.int16),
            VMEM((2, 768, 128), F32),
            VMEM((768, 256), F32),
            VMEM((R, 6, 8, 128), F32),
            VMEM((R, 8, 8, 128), F32),
            VMEM((2, 384, 128), F32),
            VMEM((3, 6, 8, 128), F32),
            VMEM((3, S, 8, 128), F32),
            VMEM((3, S, 8, 128), F32),
            VMEM((3, R, 4, 8, 128), F32),
            pltpu.SemaphoreType.DMA((8,)),
            pltpu.SemaphoreType.DMA((2,)),
            pltpu.SemaphoreType.DMA((2,)),
            pltpu.SemaphoreType.DMA((2,)),
        ],
        compiler_params=pltpu.CompilerParams(collective_id=0, has_side_effects=True, vmem_limit_bytes=50000000),
        name="fused",
    )(
        *map(
            pin,
            (
                slip_mask.reshape((2, 32)),
                slip_field.reshape((128, GRID)),
                slice_layer,
                layer_material,
                materials,
                jnp.asarray(twiddle),
                jnp.asarray(real_dft),
                jnp.asarray(complex_dft),
            ),
        )
    )
    return result.reshape((1, 32, GRID))


def solution(mesh):
    placed = (P("depth", None, "wave", None), P("depth", "wave", None), P(), P(), P())
    return jax.shard_map(
        shards, mesh=mesh, in_specs=placed, out_specs=P("depth", "wave", None), check_vma=False
    )
```
